32 devices in a mesh: ctx: 8 (over z, x), head: 4 (over y, core).
Axes of the slice: x: 2, y: 2, z: 4, core: 2. Of those that a mesh axis runs over, the one named last changes fastest.
Arguments:
- queries: bfloat16 [4096, 3072], P('ctx', 'head'), may hold values from -26 to 26
- keys: bfloat16 [4096, 3072], P('ctx', 'head'), may hold values from -26 to 26
- values: bfloat16 [4096, 3072], P('ctx', 'head'), may hold values from -6 to 6
- kv_tiles: int32 [32, 12], replicated, may hold values from 0 to 31, as said below
- out_weight: bfloat16 [3072, 3072], P('head'), may hold values from -0.109375 to 0.109375
Outputs:
- attended: bfloat16 [4096, 3072], P(('ctx', 'head'))
The draws below stay inside these ranges and needn't reach their ends.
Inputs may be any that keep to these rules, and one draw needn't show every extreme that they name: `kv_tiles`: every row i lists tile i itself; entries may repeat. A listed tile lies on a device (tile index // 4) within 2 of the device of row i, and from every other device within 2 the rows of one device read between 1 and 2 distinct tiles.
All inputs are finite; a program needn't handle non-finite values.
Results may differ from the reference program's by a relative error of at most 0.009.
Values may be sent and summed in bfloat16 or wider, within the bound.
A program may use at most 128 MiB of HBM per device.

```python
import jax
import jax.numpy as jnp
from jax import lax

HEADS = 24
HD = 128
DOUT = 3072
TILE = 128
REACH = 2
CAP = 2
QT = 4
NT = 32
MAXK = 12
TOKENS = 4096
N_HEAD = 4


def draw_queries(key, part):
    shape = (TOKENS, HEADS * HD)
    base = jnp.clip(jax.random.normal(jax.random.fold_in(key, 1), shape, dtype=jnp.float32), -4.0, 4.0)
    return base.astype(jnp.bfloat16)


def draw_keys(key, part):
    shape = (TOKENS, HEADS * HD)
    base = jnp.clip(jax.random.normal(jax.random.fold_in(key, 2), shape, dtype=jnp.float32), -4.0, 4.0)
    return base.astype(jnp.bfloat16)


def draw_kv_tiles(key, part):
    dev_count = NT // QT
    offsets = jnp.arange(2 * REACH, dtype=jnp.int32)
    offsets = jnp.where(offsets < REACH, offsets - REACH, offsets - REACH + 1)
    devices = jnp.arange(dev_count, dtype=jnp.int32)
    sources = devices[:, None] + offsets[None, :]
    in_range = (sources >= 0) & (sources < dev_count)
    heavy = jax.random.randint(jax.random.fold_in(key, 1), (dev_count, 2 * REACH), 0, 4, dtype=jnp.int32) == 0
    needed = jnp.where(heavy, CAP, 1)
    busiest = jax.random.randint(jax.random.fold_in(key, 2), (), 0, dev_count, dtype=jnp.int32)
    needed = jnp.where(devices[:, None] == busiest, CAP, needed)
    tile_local = jnp.arange(QT, dtype=jnp.int32)
    ranking = jax.random.randint(jax.random.fold_in(key, 3), (dev_count, 2 * REACH, QT), 0, 1048576, dtype=jnp.int32) * QT + tile_local
    picked = jnp.argsort(ranking, axis=-1)[:, :, :CAP].astype(jnp.int32)
    slot_ids = jnp.arange(CAP, dtype=jnp.int32)
    remote_usable = in_range[:, :, None] & (slot_ids[None, None, :] < needed[:, :, None])
    remote_ids = sources[:, :, None] * QT + picked
    own_ids = devices[:, None] * QT + tile_local[None, :]
    candidates = jnp.concatenate([own_ids, remote_ids.reshape(dev_count, 2 * REACH * CAP)], axis=1)
    usable = jnp.concatenate([jnp.ones((dev_count, QT), dtype=bool), remote_usable.reshape(dev_count, 2 * REACH * CAP)], axis=1)
    primary = jax.random.randint(jax.random.fold_in(key, 4), (dev_count, MAXK), 0, QT, dtype=jnp.int32)
    second = jax.random.randint(jax.random.fold_in(key, 5), (dev_count, MAXK), 0, 2, dtype=jnp.int32) == 1
    assigned = (primary[:, None, :] == tile_local[None, :, None]) | second[:, None, :] & (((primary + 1) % QT)[:, None, :] == tile_local[None, :, None])
    diagonal = devices[:, None] * QT + tile_local[None, :]
    entries = jnp.where(usable[:, None, :] & assigned, candidates[:, None, :], diagonal[:, :, None])
    shuffle = jax.random.randint(jax.random.fold_in(key, 6), (dev_count, QT, MAXK), 0, 1048576, dtype=jnp.int32) * MAXK + jnp.arange(MAXK, dtype=jnp.int32)
    permuted_at = jnp.argsort(shuffle, axis=-1)
    entries = jnp.take_along_axis(entries, permuted_at, axis=-1)
    return entries.reshape(NT, MAXK).astype(jnp.int32)


def block_scale(rng, extent, pieces, least, high):
    gain = 1.0
    for axis_at, blocks in pieces:
        steps = jax.random.uniform(jax.random.fold_in(jax.random.fold_in(rng, 6), axis_at), (blocks,), jnp.float32, least / len(pieces), high / len(pieces))
        gain = gain * jnp.repeat(jnp.exp(steps), extent[axis_at] // blocks).reshape((-1,) + (1,) * (len(extent) - 1 - axis_at))
    return gain


def gaussian(key, shape, width, bound, pieces=(), held_as=jnp.bfloat16):
    factor_of = block_scale(key, shape, pieces, -0.22, 0.18) if pieces else 1.0
    values = jax.random.normal(key, shape, jnp.float32) * width * factor_of
    return jnp.minimum(jnp.maximum(values, -bound), bound).astype(held_as)


def setup_inputs(seed: int = 0) -> dict:
    seeds = jax.random.split(jax.random.key(seed), 6)
    return {
        "queries": draw_queries(jax.random.fold_in(seeds[5], 71), 0),
        "keys": draw_keys(jax.random.fold_in(seeds[5], 71), 0),
        "values": gaussian(seeds[2], (TOKENS, HEADS * HD), 1.0, 6.0, ((0, 8), (1, 4))),
        "kv_tiles": draw_kv_tiles(jax.random.fold_in(seeds[5], 71), 0),
        "out_weight": gaussian(seeds[4], (HEADS * HD, DOUT), (HEADS * HD) ** -0.5, 0.109375, ((0, 4),)),
    }


def reference(queries, keys, values, kv_tiles, out_weight):
    query_tiles = queries.reshape(NT, TILE, HEADS, HD)
    key_tiles = keys.reshape(NT, TILE, HEADS * HD)
    value_tiles = values.reshape(NT, TILE, HEADS * HD)
    earlier = jnp.tril(jnp.ones((MAXK, MAXK), dtype=bool), -1)
    score_scale = HD ** -0.5

    def one_tile(tile_index):
        tile_list = kv_tiles[tile_index]
        repeated = jnp.any((tile_list[:, None] == tile_list[None, :]) & earlier, axis=1)
        key_rows = key_tiles[tile_list].reshape(MAXK * TILE, HEADS, HD).astype(jnp.float32)
        value_rows = value_tiles[tile_list].reshape(MAXK * TILE, HEADS, HD).astype(jnp.float32)
        query_rows = query_tiles[tile_index].astype(jnp.float32)
        scores = jnp.einsum("qhd,khd->hqk", query_rows, key_rows) * score_scale
        allowed = jnp.repeat(jnp.logical_not(repeated), TILE)[None, None, :]
        masked = jnp.where(allowed, scores, -jnp.inf)
        row_max = jnp.max(masked, axis=-1, keepdims=True)
        weights = jnp.where(allowed, jnp.exp(masked - row_max), 0.0)
        denominator = jnp.sum(weights, axis=-1)
        rounded = lax.optimization_barrier(weights.astype(jnp.bfloat16)).astype(jnp.float32)
        summed = jnp.einsum("hqk,khd->qhd", rounded, value_rows)
        context_rows = summed / jnp.transpose(denominator)[:, :, None]
        return context_rows.astype(jnp.bfloat16).reshape(TILE, HEADS * HD)

    context = lax.map(one_tile, jnp.arange(NT, dtype=jnp.int32)).reshape(TOKENS, HEADS * HD)
    group_width = HEADS * HD // N_HEAD
    summed_out = jnp.zeros((TOKENS, DOUT), jnp.float32)
    for group_index in range(N_HEAD):
        lower = group_index * group_width
        partial_value = jnp.dot(context[:, lower:lower + group_width], out_weight[lower:lower + group_width], preferred_element_type=jnp.float32).astype(jnp.bfloat16)
        summed_out = summed_out + partial_value.astype(jnp.float32)
    return summed_out.astype(jnp.bfloat16)
```

```python
import functools
import math

import jax
import jax.numpy as jnp
from jax import lax
from jax.experimental import pallas as pl
from jax.experimental.pallas import tpu as pltpu
from jax.sharding import PartitionSpec as P

HD = 128
TILE = 128
REACH = 2
PAIR = 2
KINDS = 2 * REACH
MASKED = -1e30
MESH = pl.DeviceIdType.MESH


def dot(a, b, contract):
    return lax.dot_general(a, b, (((1,), (contract,)), ((), ())), preferred_element_type=jnp.float32)


def kernel(devices, groups, chunk, late, lists_in, q_in, k_in, v_in, w_in, out,
           lists, q, k, v, w, bias, packed, halo, ctx, ctx_far, w_far,
           kept, sum_out, sum_in, part_out, part_in, own, own_out, own_in,
           load_sems, halo_send, halo_recv, w_send, w_recv, ctx_send, ctx_recv,
           sum_send, sum_recv, part_send, part_recv, own_send, own_recv):
    device, group = lax.axis_index("ctx"), lax.axis_index("head")
    parity, place = group % 2, group // 2
    mate = group + 1 - 2 * parity
    tokens, columns = q.shape
    heads, tiles = columns // HD, tokens // TILE
    width = out.shape[1]
    rows = tokens // groups
    block = 2 * rows
    pairs = groups // 2
    chunks = width // chunk
    most_late = max(late)
    first_late = heads - most_late

    side = device % 2
    sources = (device + 1 - 2 * side, device - 1 + 2 * side, device - 2, device + 2)
    readers = (sources[0], sources[1], device + 2, device - 2)

    def inside(index):
        return (index >= 0) & (index < devices)

    def peer(step):
        return 2 * ((place + step) % pairs) + parity

    load_lists = pltpu.make_async_copy(lists_in, lists, load_sems.at[0])
    load_k = pltpu.make_async_copy(k_in, k, load_sems.at[1])
    load_v = pltpu.make_async_copy(v_in, v, load_sems.at[2])
    load_q = pltpu.make_async_copy(q_in, q, load_sems.at[3])
    load_w = pltpu.make_async_copy(w_in, w, load_sems.at[4])
    for load in (load_lists, load_k, load_v, load_q, load_w):
        load.start()

    barrier = pltpu.get_barrier_semaphore()
    expected = jnp.int32(pairs)
    for kind in range(KINDS):
        @pl.when(inside(readers[kind]))
        def _(kind=kind):
            pl.semaphore_signal(barrier, 1, device_id=(readers[kind], group), device_id_type=MESH)
        expected = expected + inside(sources[kind]).astype(jnp.int32)
    pl.semaphore_signal(barrier, 1, device_id=(device, mate), device_id_type=MESH)
    for step in range(1, pairs):
        pl.semaphore_signal(barrier, 1, device_id=(device, peer(step)), device_id_type=MESH)

    load_lists.wait()
    entries = lists.shape[0]

    def sent(r, found):
        found = list(found)
        for kind in range(KINDS):
            row = (readers[kind] + devices) % devices * tiles + r
            for e in range(entries):
                x = lists[e, row] - device * tiles
                least, most = found[2 * kind], found[2 * kind + 1]
                found[2 * kind] = jnp.minimum(least, jnp.where(x < 0, tiles - 1, x))
                found[2 * kind + 1] = jnp.maximum(most, jnp.where(x >= tiles, 0, x))
        return tuple(found)

    ids = lax.fori_loop(0, tiles, sent, (jnp.int32(tiles - 1), jnp.int32(0)) * KINDS)

    load_k.wait()
    load_v.wait()
    pl.semaphore_wait(barrier, expected)

    def w_copy(c):
        source = w_in.at[pl.ds((heads - late[c]) * HD, late[c] * HD), pl.ds(c * chunk, chunk)]
        return pltpu.make_async_remote_copy(
            src_ref=source, dst_ref=w_far.at[c, pl.ds((most_late - late[c]) * HD, late[c] * HD)],
            send_sem=w_send.at[c], recv_sem=w_recv.at[c],
            device_id=(device, peer(1)), device_id_type=MESH)

    late_chunks = [c for c in range(chunks) if late[c]]
    for c in late_chunks:
        w_copy(c).start()

    def halo_copy(h, kind):
        return pltpu.make_async_remote_copy(
            src_ref=packed.at[h, kind], dst_ref=halo.at[h, kind],
            send_sem=halo_send.at[h, kind], recv_sem=halo_recv.at[h, kind],
            device_id=(readers[kind], group), device_id_type=MESH)

    def send_halo(h, carry):
        lanes = pl.ds(pl.multiple_of(h * HD, HD), HD)
        for kind in range(KINDS):
            for which in range(PAIR):
                picked = ids[PAIR * kind + which]
                for part, ref in ((0, k), (1, v)):
                    at = (part * PAIR + which) * TILE
                    packed[h, kind, at:at + TILE, :] = ref[picked, :, lanes]
        for kind in (3, 1, 0, 2):
            @pl.when(inside(readers[kind]))
            def _(kind=kind):
                halo_copy(h, kind).start()
        return carry

    lax.fori_loop(0, heads, send_halo, 0)

    for kind in range(KINDS):
        @pl.when(jnp.logical_not(inside(sources[kind])))
        def _(kind=kind):
            halo[:, kind] = jnp.zeros((heads,) + halo.shape[2:], halo.dtype)

    def received(r, found):
        found = list(found)
        for e in range(entries):
            tile = lists[e, device * tiles + r]
            for kind in range(KINDS):
                x = tile - sources[kind] * tiles
                least, most = found[2 * kind], found[2 * kind + 1]
                found[2 * kind] = jnp.minimum(least, jnp.where(x < 0, tiles, x))
                found[2 * kind + 1] = jnp.maximum(most, jnp.where(x >= tiles, -1, x))
        return tuple(found)

    found = lax.fori_loop(0, tiles, received, (jnp.int32(tiles), jnp.int32(-1)) * KINDS)
    listed = [device * tiles + j for j in range(tiles)]
    for kind in range(KINDS):
        least, most = found[2 * kind], found[2 * kind + 1]
        listed.append(jnp.where(least < tiles, sources[kind] * tiles + least, -1))
        listed.append(jnp.where(most > least, sources[kind] * tiles + most, -1))

    def mask(t, carry):
        added = [jnp.float32(MASKED)] * len(listed)
        for e in range(entries):
            tile = lists[e, device * tiles + t]
            added = [jnp.where(tile == other, 0.0, value) for other, value in zip(listed, added)]
        for j, value in enumerate(added):
            bias[t, :, j * TILE:(j + 1) * TILE] = jnp.full((1, TILE), value, jnp.float32)
        return carry

    lax.fori_loop(0, tiles, mask, 0)
    load_q.wait()
    load_w.wait()

    scale = HD ** -0.5 * math.log2(math.e)
    near = tokens

    def block_start(step):
        return pl.multiple_of((place + step) % pairs * block, block)

    def attend(h, lanes, first):
        span = pl.ds(pl.multiple_of(first, TILE), TILE)
        k_own, v_own = k[:, :, lanes].reshape(tokens, HD), v[:, :, lanes].reshape(tokens, HD)
        k_far = halo[h, :, :PAIR * TILE].reshape(KINDS * PAIR * TILE, HD)
        v_far = halo[h, :, PAIR * TILE:].reshape(KINDS * PAIR * TILE, HD)
        qt = q[span, lanes]
        shift = bias[first // TILE]
        s_own = dot(qt, k_own, 1) * scale + shift[:, :near]
        s_far = dot(qt, k_far, 1) * scale + shift[:, near:]
        top = jnp.maximum(jnp.max(s_own, axis=1, keepdims=True), jnp.max(s_far, axis=1, keepdims=True))
        p_own, p_far = jnp.exp2(s_own - top), jnp.exp2(s_far - top)
        total = jnp.sum(p_own, axis=1, keepdims=True) + jnp.sum(p_far, axis=1, keepdims=True)
        summed = dot(p_own.astype(jnp.bfloat16), v_own, 0) + dot(p_far.astype(jnp.bfloat16), v_far, 0)
        ctx[span, lanes] = (summed * (1.0 / total)).astype(ctx.dtype)

    def halves(whole):
        low, high = whole[:rows], whole[rows:]
        return jnp.where(parity == 0, low, high), jnp.where(parity == 0, high, low)

    def sum_copy(step, c):
        return pltpu.make_async_remote_copy(
            src_ref=sum_out.at[step - 1, c], dst_ref=sum_in.at[step - 1, c],
            send_sem=sum_send.at[step - 1, c], recv_sem=sum_recv.at[step - 1, c],
            device_id=(device, mate), device_id_type=MESH)

    def part_copy(step, c):
        return pltpu.make_async_remote_copy(
            src_ref=part_out.at[step - 1, c], dst_ref=part_in.at[step - 1, c],
            send_sem=part_send.at[step - 1, c], recv_sem=part_recv.at[step - 1, c],
            device_id=(device, peer(step)), device_id_type=MESH)

    def own_copy(c):
        return pltpu.make_async_remote_copy(
            src_ref=own_out.at[c], dst_ref=own_in.at[c],
            send_sem=own_send.at[c], recv_sem=own_recv.at[c],
            device_id=(device, mate), device_id_type=MESH)

    def ctx_copy(j):
        lanes = pl.ds(pl.multiple_of((first_late + j) * HD, HD), HD)
        return pltpu.make_async_remote_copy(
            src_ref=ctx.at[pl.ds(block_start(1), block), lanes],
            dst_ref=ctx_far.at[:, pl.ds(pl.multiple_of(j * HD, HD), HD)],
            send_sem=ctx_send.at[j], recv_sem=ctx_recv.at[j],
            device_id=(device, peer(1)), device_id_type=MESH)

    stages = [(count, [(step, c) for step in range(1, pairs) for c in range(chunks) if late[c] == count])
              for count in sorted(set(late), reverse=True)]

    def project(count, ready):
        depth = (heads - count) * HD
        for step, c in ready:
            whole = dot(ctx[pl.ds(block_start(step), block), :depth], w[:depth, c * chunk:(c + 1) * chunk], 0)
            mine, other = halves(whole)
            kept[step - 1, c] = mine
            sum_out[step - 1, c] = other.astype(sum_out.dtype)
            sum_copy(step, c).start()

    def forward(ready):
        for step, c in ready:
            sum_copy(step, c).wait_recv()
            part_out[step - 1, c] = (kept[step - 1, c] + sum_in[step - 1, c].astype(jnp.float32)).astype(part_out.dtype)
            part_copy(step, c).start()

    def one_head(h, carry):
        for kind in range(KINDS):
            @pl.when(inside(sources[kind]))
            def _(kind=kind):
                halo_copy(h, kind).wait_recv()
        lanes = pl.ds(pl.multiple_of(h * HD, HD), HD)
        for step in range(1, pairs):
            for j in range(block // TILE):
                attend(h, lanes, block_start(step) + j * TILE)
        for count, ready in stages:
            @pl.when(h == heads - 1 - count)
            def _(count=count, ready=ready):
                project(count, ready)
        if most_late:
            @pl.when(h >= first_late)
            def _():
                ctx_copy(h - first_late).start()
        for j in range(block // TILE):
            attend(h, lanes, block_start(0) + j * TILE)
        for count, ready in stages:
            @pl.when(h == heads - 1 - count)
            def _(count=count, ready=ready):
                forward(ready)
        return carry

    lax.fori_loop(0, heads, one_head, 0)

    mine_rows = pl.ds(block_start(0), block)
    for c in range(chunks):
        own[c] = dot(ctx[mine_rows, :], w[:, c * chunk:(c + 1) * chunk], 0)
    for c in late_chunks:
        w_copy(c).wait_recv()
    for j in range(most_late):
        ctx_copy(j).wait_recv()
    for c in range(chunks):
        whole = own[c]
        if late[c]:
            skip = (most_late - late[c]) * HD
            whole = whole + dot(ctx_far[:, skip:], w_far[c, skip:, :], 0)
        mine, other = halves(whole)
        own[c, :rows] = mine
        own_out[c] = other.astype(own_out.dtype)
        own_copy(c).start()
    for _, ready in stages:
        for c in [c for step, c in ready if step == 1]:
            own_copy(c).wait_recv()
            total = own[c, :rows] + own_in[c].astype(jnp.float32)
            for step in range(1, pairs):
                part_copy(step, c).wait_recv()
                total = total + part_in[step - 1, c].astype(jnp.float32)
            out[:, c * chunk:(c + 1) * chunk] = total.astype(out.dtype)

    def drain_halo(h, carry):
        for kind in range(KINDS):
            @pl.when(inside(readers[kind]))
            def _(kind=kind):
                halo_copy(h, kind).wait_send()
        return carry
    lax.fori_loop(0, heads, drain_halo, 0)
    for c in late_chunks:
        w_copy(c).wait_send()
    for j in range(most_late):
        ctx_copy(j).wait_send()
    for c in range(chunks):
        own_copy(c).wait_send()
        for step in range(1, pairs):
            sum_copy(step, c).wait_send()
            part_copy(step, c).wait_send()


def lateness(heads, pairs, chunks):
    if pairs != 2 or heads < 3:
        return (0,) * chunks
    return tuple(2 if 2 * c < chunks else 1 for c in range(chunks))


def body(queries, keys, values, kv_tiles, out_weight):
    tokens, columns = queries.shape
    width = out_weight.shape[1]
    devices, groups = lax.axis_size("ctx"), lax.axis_size("head")
    heads, rows, pairs = columns // HD, tokens // groups, groups // 2
    chunk = min(width, 512)
    chunks = width // chunk
    late = lateness(heads, pairs, chunks)
    deep = max(max(late), 1)
    sems = pltpu.SemaphoreType.DMA
    bf16, f32 = jnp.bfloat16, jnp.float32
    operands = (kv_tiles.T, queries, keys.reshape(-1, TILE, columns), values.reshape(-1, TILE, columns), out_weight)
    return pl.pallas_call(
        functools.partial(kernel, devices, groups, chunk, late),
        out_shape=jax.ShapeDtypeStruct((rows, width), bf16),
        in_specs=[pl.BlockSpec(memory_space=pltpu.HBM)] * len(operands),
        out_specs=pl.BlockSpec(memory_space=pltpu.VMEM),
        scratch_shapes=[
            pltpu.SMEM(kv_tiles.shape[::-1], jnp.int32),
            pltpu.VMEM((tokens, columns), bf16),
            pltpu.VMEM((tokens // TILE, TILE, columns), bf16),
            pltpu.VMEM((tokens // TILE, TILE, columns), bf16),
            pltpu.VMEM((columns, width), bf16),
            pltpu.VMEM((tokens // TILE, 1, tokens + KINDS * PAIR * TILE), f32),
            pltpu.VMEM((heads, KINDS, 2 * PAIR * TILE, HD), bf16),
            pltpu.VMEM((heads, KINDS, 2 * PAIR * TILE, HD), bf16),
            pltpu.VMEM((tokens, columns), bf16),
            pltpu.VMEM((2 * rows, deep * HD), bf16),
            pltpu.VMEM((chunks, deep * HD, chunk), bf16),
            pltpu.VMEM((pairs - 1, chunks, rows, chunk), f32),
            pltpu.VMEM((pairs - 1, chunks, rows, chunk), bf16),
            pltpu.VMEM((pairs - 1, chunks, rows, chunk), bf16),
            pltpu.VMEM((pairs - 1, chunks, rows, chunk), bf16),
            pltpu.VMEM((pairs - 1, chunks, rows, chunk), bf16),
            pltpu.VMEM((chunks, 2 * rows, chunk), f32),
            pltpu.VMEM((chunks, rows, chunk), bf16),
            pltpu.VMEM((chunks, rows, chunk), bf16),
            sems((5,)),
            sems((heads, KINDS)), sems((heads, KINDS)),
            sems((chunks,)), sems((chunks,)),
            sems((deep,)), sems((deep,)),
            sems((pairs - 1, chunks)), sems((pairs - 1, chunks)),
            sems((pairs - 1, chunks)), sems((pairs - 1, chunks)),
            sems((chunks,)), sems((chunks,)),
        ],
        compiler_params=pltpu.CompilerParams(
            collective_id=0, has_side_effects=True, vmem_limit_bytes=40 * 2 ** 20),
    )(*[pltpu.with_memory_space_constraint(operand, pltpu.HBM) for operand in operands])


def solution(mesh):
    return jax.shard_map(
        body,
        mesh=mesh,
        in_specs=(P("ctx", "head"), P("ctx", "head"), P("ctx", "head"), P(), P("head", None)),
        out_specs=P(("ctx", "head"), None),
        check_vma=False,
    )
```

```python
import functools
import math

import jax
import jax.numpy as jnp
from jax import lax
from jax.experimental import pallas as pl
from jax.experimental.pallas import tpu as pltpu
from jax.sharding import PartitionSpec as P

HD = 128
TILE = 128
REACH = 2
PAIR = 2
KINDS = 2 * REACH
MASKED = -1e30
LAG = 3
HOLD = 2
MESH = pl.DeviceIdType.MESH


def dot(a, b, contract):
    return lax.dot_general(a, b, (((1,), (contract,)), ((), ())), preferred_element_type=jnp.float32)


def kernel(devices, groups, chunk, late, lists_in, q_in, k_in, v_in, w_in, out,
           lists, q, k, v, w, bias, packed, halo, ctx, ctx_far, w_far,
           kept, sum_out, sum_in, part_out, part_in, own, own_out, own_in,
           load_sems, halo_send, halo_recv, w_send, w_recv, ctx_send, ctx_recv,
           sum_send, sum_recv, part_send, part_recv, own_send, own_recv):
    device, group = lax.axis_index("ctx"), lax.axis_index("head")
    parity, place = group % 2, group // 2
    mate = group + 1 - 2 * parity
    tokens, columns = q.shape
    heads, tiles = columns // HD, tokens // TILE
    width = out.shape[1]
    rows = tokens // groups
    block = 2 * rows
    pairs = groups // 2
    chunks = width // chunk
    most_late = max(late)
    first_late = heads - most_late

    side = device % 2
    sources = (device + 1 - 2 * side, device - 1 + 2 * side, device - 2, device + 2)
    readers = (sources[0], sources[1], device + 2, device - 2)

    def inside(index):
        return (index >= 0) & (index < devices)

    def peer(step):
        return 2 * ((place + step) % pairs) + parity

    load_lists = pltpu.make_async_copy(lists_in, lists, load_sems.at[0])
    load_k = pltpu.make_async_copy(k_in, k, load_sems.at[1])
    load_v = pltpu.make_async_copy(v_in, v, load_sems.at[2])
    load_q = pltpu.make_async_copy(q_in, q, load_sems.at[3])
    load_w = pltpu.make_async_copy(w_in, w, load_sems.at[4])
    for load in (load_lists, load_k, load_v, load_q, load_w):
        load.start()

    barrier = pltpu.get_barrier_semaphore()
    expected = jnp.int32(pairs)
    for kind in range(KINDS):
        @pl.when(inside(readers[kind]))
        def _(kind=kind):
            pl.semaphore_signal(barrier, 1, device_id=(readers[kind], group), device_id_type=MESH)
        expected = expected + inside(sources[kind]).astype(jnp.int32)
    pl.semaphore_signal(barrier, 1, device_id=(device, mate), device_id_type=MESH)
    for step in range(1, pairs):
        pl.semaphore_signal(barrier, 1, device_id=(device, peer(step)), device_id_type=MESH)

    load_lists.wait()
    entries = lists.shape[0]

    def sent(r, found):
        found = list(found)
        for kind in range(KINDS):
            row = (readers[kind] + devices) % devices * tiles + r
            for e in range(entries):
                x = lists[e, row] - device * tiles
                least, most = found[2 * kind], found[2 * kind + 1]
                found[2 * kind] = jnp.minimum(least, jnp.where(x < 0, tiles - 1, x))
                found[2 * kind + 1] = jnp.maximum(most, jnp.where(x >= tiles, 0, x))
        return tuple(found)

    ids = lax.fori_loop(0, tiles, sent, (jnp.int32(tiles - 1), jnp.int32(0)) * KINDS)

    load_k.wait()
    load_v.wait()
    pl.semaphore_wait(barrier, expected)

    def w_copy(c):
        source = w_in.at[pl.ds((heads - late[c]) * HD, late[c] * HD), pl.ds(c * chunk, chunk)]
        return pltpu.make_async_remote_copy(
            src_ref=source, dst_ref=w_far.at[c, pl.ds((most_late - late[c]) * HD, late[c] * HD)],
            send_sem=w_send.at[c], recv_sem=w_recv.at[c],
            device_id=(device, peer(1)), device_id_type=MESH)

    late_chunks = [c for c in range(chunks) if late[c]]
    for c in late_chunks:
        w_copy(c).start()

    def halo_copy(h, kind):
        return pltpu.make_async_remote_copy(
            src_ref=packed.at[h, kind], dst_ref=halo.at[h, kind],
            send_sem=halo_send.at[h, kind], recv_sem=halo_recv.at[h, kind],
            device_id=(readers[kind], group), device_id_type=MESH)

    def send_halo(h, carry):
        lanes = pl.ds(pl.multiple_of(h * HD, HD), HD)
        for kind in range(KINDS):
            for which in range(PAIR):
                picked = ids[PAIR * kind + which]
                for part, ref in ((0, k), (1, v)):
                    at = (part * PAIR + which) * TILE
                    packed[h, kind, at:at + TILE, :] = ref[picked, :, lanes]
        for kind in (3, 1, 0, 2):
            @pl.when(inside(readers[kind]))
            def _(kind=kind):
                halo_copy(h, kind).start()
        return carry

    lax.fori_loop(0, heads, send_halo, 0)

    for kind in range(KINDS):
        @pl.when(jnp.logical_not(inside(sources[kind])))
        def _(kind=kind):
            halo[:, kind] = jnp.zeros((heads,) + halo.shape[2:], halo.dtype)

    def received(r, found):
        found = list(found)
        for e in range(entries):
            tile = lists[e, device * tiles + r]
            for kind in range(KINDS):
                x = tile - sources[kind] * tiles
                least, most = found[2 * kind], found[2 * kind + 1]
                found[2 * kind] = jnp.minimum(least, jnp.where(x < 0, tiles, x))
                found[2 * kind + 1] = jnp.maximum(most, jnp.where(x >= tiles, -1, x))
        return tuple(found)

    found = lax.fori_loop(0, tiles, received, (jnp.int32(tiles), jnp.int32(-1)) * KINDS)
    listed = [device * tiles + j for j in range(tiles)]
    for kind in range(KINDS):
        least, most = found[2 * kind], found[2 * kind + 1]
        listed.append(jnp.where(least < tiles, sources[kind] * tiles + least, -1))
        listed.append(jnp.where(most > least, sources[kind] * tiles + most, -1))

    def mask(t, carry):
        added = [jnp.float32(MASKED)] * len(listed)
        for e in range(entries):
            tile = lists[e, device * tiles + t]
            added = [jnp.where(tile == other, 0.0, value) for other, value in zip(listed, added)]
        for j, value in enumerate(added):
            bias[t, :, j * TILE:(j + 1) * TILE] = jnp.full((1, TILE), value, jnp.float32)
        return carry

    lax.fori_loop(0, tiles, mask, 0)
    load_q.wait()
    load_w.wait()

    scale = HD ** -0.5 * math.log2(math.e)
    near = tokens

    def block_start(step):
        return pl.multiple_of((place + step) % pairs * block, block)

    def attend(h, lanes, first):
        span = pl.ds(pl.multiple_of(first, TILE), TILE)
        k_own, v_own = k[:, :, lanes].reshape(tokens, HD), v[:, :, lanes].reshape(tokens, HD)
        k_far = halo[h, :, :PAIR * TILE].reshape(KINDS * PAIR * TILE, HD)
        v_far = halo[h, :, PAIR * TILE:].reshape(KINDS * PAIR * TILE, HD)
        qt = q[span, lanes]
        shift = bias[first // TILE]
        s_own = dot(qt, k_own, 1) * scale + shift[:, :near]
        s_far = dot(qt, k_far, 1) * scale + shift[:, near:]
        top = jnp.maximum(jnp.max(s_own, axis=1, keepdims=True), jnp.max(s_far, axis=1, keepdims=True))
        p_own, p_far = jnp.exp2(s_own - top), jnp.exp2(s_far - top)
        total = jnp.sum(p_own, axis=1, keepdims=True) + jnp.sum(p_far, axis=1, keepdims=True)
        summed = dot(p_own.astype(jnp.bfloat16), v_own, 0) + dot(p_far.astype(jnp.bfloat16), v_far, 0)
        ctx[span, lanes] = (summed * (1.0 / total)).astype(ctx.dtype)

    def halves(whole):
        low, high = whole[:rows], whole[rows:]
        return jnp.where(parity == 0, low, high), jnp.where(parity == 0, high, low)

    def sum_copy(step, c):
        return pltpu.make_async_remote_copy(
            src_ref=sum_out.at[step - 1, c], dst_ref=sum_in.at[step - 1, c],
            send_sem=sum_send.at[step - 1, c], recv_sem=sum_recv.at[step - 1, c],
            device_id=(device, mate), device_id_type=MESH)

    def part_copy(step, c):
        return pltpu.make_async_remote_copy(
            src_ref=part_out.at[step - 1, c], dst_ref=part_in.at[step - 1, c],
            send_sem=part_send.at[step - 1, c], recv_sem=part_recv.at[step - 1, c],
            device_id=(device, peer(step)), device_id_type=MESH)

    def own_copy(c):
        return pltpu.make_async_remote_copy(
            src_ref=own_out.at[c], dst_ref=own_in.at[c],
            send_sem=own_send.at[c], recv_sem=own_recv.at[c],
            device_id=(device, mate), device_id_type=MESH)

    def ctx_copy(j):
        lanes = pl.ds(pl.multiple_of((first_late + j) * HD, HD), HD)
        return pltpu.make_async_remote_copy(
            src_ref=ctx.at[pl.ds(block_start(1), block), lanes],
            dst_ref=ctx_far.at[:, pl.ds(pl.multiple_of(j * HD, HD), HD)],
            send_sem=ctx_send.at[j], recv_sem=ctx_recv.at[j],
            device_id=(device, peer(1)), device_id_type=MESH)

    stages = [(count, [(step, c) for step in range(1, pairs) for c in range(chunks) if late[c] == count])
              for count in sorted(set(late), reverse=True)]

    held = stages[-1][1][-HOLD:] if most_late and HOLD else []

    def project(count, ready):
        depth = (heads - count) * HD
        for at, (step, c) in enumerate(ready):
            if at >= LAG:
                forward([x for x in ready[at - LAG:at - LAG + 1] if x not in held])
            whole = dot(ctx[pl.ds(block_start(step), block), :depth], w[:depth, c * chunk:(c + 1) * chunk], 0)
            mine, other = halves(whole)
            kept[step - 1, c] = mine
            sum_out[step - 1, c] = other.astype(sum_out.dtype)
            sum_copy(step, c).start()
        forward([x for x in ready[-LAG:] if x not in held])

    def forward(ready):
        for step, c in ready:
            sum_copy(step, c).wait_recv()
            part_out[step - 1, c] = (kept[step - 1, c] + sum_in[step - 1, c].astype(jnp.float32)).astype(part_out.dtype)
            part_copy(step, c).start()

    def one_head(h, carry):
        for kind in range(KINDS):
            @pl.when(inside(sources[kind]))
            def _(kind=kind):
                halo_copy(h, kind).wait_recv()
        lanes = pl.ds(pl.multiple_of(h * HD, HD), HD)
        for step in range(1, pairs):
            for j in range(block // TILE):
                attend(h, lanes, block_start(step) + j * TILE)
        if most_late:
            @pl.when(h >= first_late)
            def _():
                ctx_copy(h - first_late).start()
        for count, ready in stages:
            @pl.when(h == heads - 1 - count)
            def _(count=count, ready=ready):
                project(count, ready)
        if held:
            @pl.when(h == heads - 1)
            def _():
                forward(held)
        for j in range(block // TILE):
            attend(h, lanes, block_start(0) + j * TILE)
        return carry

    lax.fori_loop(0, heads, one_head, 0)

    mine_rows = pl.ds(block_start(0), block)
    for c in range(chunks):
        own[c] = dot(ctx[mine_rows, :], w[:, c * chunk:(c + 1) * chunk], 0)
    for c in late_chunks:
        w_copy(c).wait_recv()
    for j in range(most_late):
        ctx_copy(j).wait_recv()
    for c in range(chunks):
        whole = own[c]
        if late[c]:
            skip = (most_late - late[c]) * HD
            whole = whole + dot(ctx_far[:, skip:], w_far[c, skip:, :], 0)
        mine, other = halves(whole)
        own[c, :rows] = mine
        own_out[c] = other.astype(own_out.dtype)
        own_copy(c).start()
    for _, ready in stages:
        for c in [c for step, c in ready if step == 1]:
            own_copy(c).wait_recv()
            total = own[c, :rows] + own_in[c].astype(jnp.float32)
            for step in range(1, pairs):
                part_copy(step, c).wait_recv()
                total = total + part_in[step - 1, c].astype(jnp.float32)
            out[:, c * chunk:(c + 1) * chunk] = total.astype(out.dtype)

    def drain_halo(h, carry):
        for kind in range(KINDS):
            @pl.when(inside(readers[kind]))
            def _(kind=kind):
                halo_copy(h, kind).wait_send()
        return carry
    lax.fori_loop(0, heads, drain_halo, 0)
    for c in late_chunks:
        w_copy(c).wait_send()
    for j in range(most_late):
        ctx_copy(j).wait_send()
    for c in range(chunks):
        own_copy(c).wait_send()
        for step in range(1, pairs):
            sum_copy(step, c).wait_send()
            part_copy(step, c).wait_send()


def lateness(heads, pairs, chunks):
    if pairs != 2 or heads < 3:
        return (0,) * chunks
    return tuple(2 if 2 * c < chunks else 1 for c in range(chunks))


def body(queries, keys, values, kv_tiles, out_weight):
    tokens, columns = queries.shape
    width = out_weight.shape[1]
    devices, groups = lax.axis_size("ctx"), lax.axis_size("head")
    heads, rows, pairs = columns // HD, tokens // groups, groups // 2
    chunk = min(width, 512)
    chunks = width // chunk
    late = lateness(heads, pairs, chunks)
    deep = max(max(late), 1)
    sems = pltpu.SemaphoreType.DMA
    bf16, f32 = jnp.bfloat16, jnp.float32
    operands = (kv_tiles.T, queries, keys.reshape(-1, TILE, columns), values.reshape(-1, TILE, columns), out_weight)
    return pl.pallas_call(
        functools.partial(kernel, devices, groups, chunk, late),
        out_shape=jax.ShapeDtypeStruct((rows, width), bf16),
        in_specs=[pl.BlockSpec(memory_space=pltpu.HBM)] * len(operands),
        out_specs=pl.BlockSpec(memory_space=pltpu.VMEM),
        scratch_shapes=[
            pltpu.SMEM(kv_tiles.shape[::-1], jnp.int32),
            pltpu.VMEM((tokens, columns), bf16),
            pltpu.VMEM((tokens // TILE, TILE, columns), bf16),
            pltpu.VMEM((tokens // TILE, TILE, columns), bf16),
            pltpu.VMEM((columns, width), bf16),
            pltpu.VMEM((tokens // TILE, 1, tokens + KINDS * PAIR * TILE), f32),
            pltpu.VMEM((heads, KINDS, 2 * PAIR * TILE, HD), bf16),
            pltpu.VMEM((heads, KINDS, 2 * PAIR * TILE, HD), bf16),
            pltpu.VMEM((tokens, columns), bf16),
            pltpu.VMEM((2 * rows, deep * HD), bf16),
            pltpu.VMEM((chunks, deep * HD, chunk), bf16),
            pltpu.VMEM((pairs - 1, chunks, rows, chunk), f32),
            pltpu.VMEM((pairs - 1, chunks, rows, chunk), bf16),
            pltpu.VMEM((pairs - 1, chunks, rows, chunk), bf16),
            pltpu.VMEM((pairs - 1, chunks, rows, chunk), bf16),
            pltpu.VMEM((pairs - 1, chunks, rows, chunk), bf16),
            pltpu.VMEM((chunks, 2 * rows, chunk), f32),
            pltpu.VMEM((chunks, rows, chunk), bf16),
            pltpu.VMEM((chunks, rows, chunk), bf16),
            sems((5,)),
            sems((heads, KINDS)), sems((heads, KINDS)),
            sems((chunks,)), sems((chunks,)),
            sems((deep,)), sems((deep,)),
            sems((pairs - 1, chunks)), sems((pairs - 1, chunks)),
            sems((pairs - 1, chunks)), sems((pairs - 1, chunks)),
            sems((chunks,)), sems((chunks,)),
        ],
        compiler_params=pltpu.CompilerParams(
            collective_id=0, has_side_effects=True, vmem_limit_bytes=40 * 2 ** 20),
    )(*[pltpu.with_memory_space_constraint(operand, pltpu.HBM) for operand in operands])


def solution(mesh):
    return jax.shard_map(
        body,
        mesh=mesh,
        in_specs=(P("ctx", "head"), P("ctx", "head"), P("ctx", "head"), P(), P("head", None)),
        out_specs=P(("ctx", "head"), None),
        check_vma=False,
    )
```

```python
import functools
import math

import jax
import jax.numpy as jnp
from jax import lax
from jax.experimental import pallas as pl
from jax.experimental.pallas import tpu as pltpu
from jax.sharding import PartitionSpec as P

HD = 128
TILE = 128
REACH = 2
PAIR = 2
KINDS = 2 * REACH
MASKED = -1e30
HOLD = 2
QUARTERS = 4
LEAD = 0
AHEAD = 1
MESH = pl.DeviceIdType.MESH


def dot(a, b, contract):
    return lax.dot_general(a, b, (((1,), (contract,)), ((), ())), preferred_element_type=jnp.float32)


def kernel(devices, groups, chunk, late, lists_in, q_in, k_in, v_in, w_in, out,
           lists, q, k, v, w, bias, packed, halo, passing, ctx, ctx_far, w_far,
           kept, sum_out, sum_in, part_out, part_in, own, own_out, own_in,
           load_sems, halo_send, halo_recv, turn_send, turn_recv, pass_send, pass_recv, w_send, w_recv, ctx_send, ctx_recv,
           sum_send, sum_recv, part_send, part_recv, own_send, own_recv):
    device, group = lax.axis_index("ctx"), lax.axis_index("head")
    parity, place = group % 2, group // 2
    mate = group + 1 - 2 * parity
    tokens, columns = q.shape
    heads, tiles = columns // HD, tokens // TILE
    width = out.shape[1]
    rows = tokens // groups
    block = 2 * rows
    pairs = groups // 2
    chunks = width // chunk
    most_late = max(late)
    first_late = heads - most_late

    side = device % 2
    sources = (device + 1 - 2 * side, device - 1 + 2 * side, device - 2, device + 2)
    readers = (sources[0], sources[1], device + 2, device - 2)

    near_kind = 1
    quarter = 2 * PAIR * TILE // QUARTERS
    layers, layer = devices // 2, device // 2
    hop = device + 2 - 4 * side

    def inside(index):
        return (index >= 0) & (index < devices)

    def turned(side, layer):
        return jnp.where(side == 1, layers - 1 - layer, layer) * QUARTERS // layers

    turned_mine, turned_passing = turned(side, layer), turned(1 - side, layer)
    turned_source = turned(1 - side, layer - 1 + 2 * side)

    def by_count(condition, count, act):
        for n in range(QUARTERS):
            @pl.when(condition & (count == n))
            def _(n=n):
                act(n)

    def peer(step):
        return 2 * ((place + step) % pairs) + parity

    load_lists = pltpu.make_async_copy(lists_in, lists, load_sems.at[0])
    load_k = pltpu.make_async_copy(k_in, k, load_sems.at[1])
    load_v = pltpu.make_async_copy(v_in, v, load_sems.at[2])
    load_q = pltpu.make_async_copy(q_in, q, load_sems.at[3])
    load_w = pltpu.make_async_copy(w_in, w, load_sems.at[4])
    for load in (load_lists, load_k, load_v, load_q, load_w):
        load.start()

    barrier = pltpu.get_barrier_semaphore()
    expected = jnp.int32(pairs)
    for kind in range(KINDS):
        @pl.when(inside(readers[kind]))
        def _(kind=kind):
            pl.semaphore_signal(barrier, 1, device_id=(readers[kind], group), device_id_type=MESH)
        expected = expected + inside(sources[kind]).astype(jnp.int32)
    pl.semaphore_signal(barrier, 1, device_id=(device, mate), device_id_type=MESH)
    for step in range(1, pairs):
        pl.semaphore_signal(barrier, 1, device_id=(device, peer(step)), device_id_type=MESH)

    load_lists.wait()
    entries = lists.shape[0]

    def sent(r, found):
        found = list(found)
        for kind in range(KINDS):
            row = (readers[kind] + devices) % devices * tiles + r
            for e in range(entries):
                x = lists[e, row] - device * tiles
                least, most = found[2 * kind], found[2 * kind + 1]
                found[2 * kind] = jnp.minimum(least, jnp.where(x < 0, tiles - 1, x))
                found[2 * kind + 1] = jnp.maximum(most, jnp.where(x >= tiles, 0, x))
        return tuple(found)

    ids = lax.fori_loop(0, tiles, sent, (jnp.int32(tiles - 1), jnp.int32(0)) * KINDS)

    load_k.wait()
    load_v.wait()
    pl.semaphore_wait(barrier, expected)

    def w_copy(c):
        source = w_in.at[pl.ds((heads - late[c]) * HD, late[c] * HD), pl.ds(c * chunk, chunk)]
        return pltpu.make_async_remote_copy(
            src_ref=source, dst_ref=w_far.at[c, pl.ds((most_late - late[c]) * HD, late[c] * HD)],
            send_sem=w_send.at[c], recv_sem=w_recv.at[c],
            device_id=(device, peer(1)), device_id_type=MESH)

    late_chunks = [c for c in range(chunks) if late[c]]
    for c in late_chunks:
        w_copy(c).start()

    def halo_copy(h, kind):
        return pltpu.make_async_remote_copy(
            src_ref=packed.at[h, kind], dst_ref=halo.at[h, kind],
            send_sem=halo_send.at[h, kind], recv_sem=halo_recv.at[h, kind],
            device_id=(readers[kind], group), device_id_type=MESH)

    def direct_copy(h, n):
        span = pl.ds(n * quarter, (QUARTERS - n) * quarter)
        return pltpu.make_async_remote_copy(
            src_ref=packed.at[h, near_kind, span], dst_ref=halo.at[h, near_kind, span],
            send_sem=halo_send.at[h, near_kind], recv_sem=halo_recv.at[h, near_kind],
            device_id=(readers[near_kind], group), device_id_type=MESH)

    def turn_copy(h, n):
        span = pl.ds(0, n * quarter)
        return pltpu.make_async_remote_copy(
            src_ref=packed.at[h, near_kind, span], dst_ref=passing.at[h, span],
            send_sem=turn_send.at[h], recv_sem=turn_recv.at[h],
            device_id=(readers[0], group), device_id_type=MESH)

    def pass_copy(h, n):
        span = pl.ds(0, n * quarter)
        return pltpu.make_async_remote_copy(
            src_ref=passing.at[h, span], dst_ref=halo.at[h, near_kind, span],
            send_sem=pass_send.at[h], recv_sem=pass_recv.at[h],
            device_id=(hop, group), device_id_type=MESH)

    def pass_on(h):
        def one(n):
            if n:
                turn_copy(h, n).wait_recv()
                pass_copy(h, n).start()
        by_count(inside(hop), turned_passing, one)

    def pack(h, kinds):
        lanes = pl.ds(pl.multiple_of(h * HD, HD), HD)
        for kind in kinds:
            for which in range(PAIR):
                picked = ids[PAIR * kind + which]
                for part, ref in ((0, k), (1, v)):
                    at = (part * PAIR + which) * TILE
                    packed[h, kind, at:at + TILE, :] = ref[picked, :, lanes]

    def send_turn(h):
        pack(h, (near_kind,))
        by_count(inside(readers[near_kind]), turned_mine, lambda n: turn_copy(h, n).start() if n else None)

    def send_rest(h):
        pack(h, [kind for kind in range(KINDS) if kind != near_kind])
        for kind in (3, near_kind, 0, 2):
            if kind == near_kind:
                by_count(inside(readers[kind]), turned_mine, lambda n: direct_copy(h, n).start())
                continue

            @pl.when(inside(readers[kind]))
            def _(kind=kind):
                halo_copy(h, kind).start()

    ahead = min(AHEAD, heads)
    lead = min(ahead + LEAD, heads) - ahead
    for h in range(lead):
        send_turn(h)
    for h in range(ahead):
        if h + lead < heads:
            send_turn(h + lead)
        send_rest(h)

    for kind in range(KINDS):
        @pl.when(jnp.logical_not(inside(sources[kind])))
        def _(kind=kind):
            halo[:, kind] = jnp.zeros((heads,) + halo.shape[2:], halo.dtype)

    def received(r, found):
        found = list(found)
        for e in range(entries):
            tile = lists[e, device * tiles + r]
            for kind in range(KINDS):
                x = tile - sources[kind] * tiles
                least, most = found[2 * kind], found[2 * kind + 1]
                found[2 * kind] = jnp.minimum(least, jnp.where(x < 0, tiles, x))
                found[2 * kind + 1] = jnp.maximum(most, jnp.where(x >= tiles, -1, x))
        return tuple(found)

    found = lax.fori_loop(0, tiles, received, (jnp.int32(tiles), jnp.int32(-1)) * KINDS)
    listed = [device * tiles + j for j in range(tiles)]
    for kind in range(KINDS):
        least, most = found[2 * kind], found[2 * kind + 1]
        listed.append(jnp.where(least < tiles, sources[kind] * tiles + least, -1))
        listed.append(jnp.where(most > least, sources[kind] * tiles + most, -1))

    def mask(t, carry):
        added = [jnp.float32(MASKED)] * len(listed)
        for e in range(entries):
            tile = lists[e, device * tiles + t]
            added = [jnp.where(tile == other, 0.0, value) for other, value in zip(listed, added)]
        for j, value in enumerate(added):
            bias[t, :, j * TILE:(j + 1) * TILE] = jnp.full((1, TILE), value, jnp.float32)
        return carry

    lax.fori_loop(0, tiles, mask, 0)
    load_q.wait()
    load_w.wait()

    scale = HD ** -0.5 * math.log2(math.e)
    near = tokens

    def block_start(step):
        return pl.multiple_of((place + step) % pairs * block, block)

    def attend(h, lanes, first):
        span = pl.ds(pl.multiple_of(first, TILE), block)
        k_own, v_own = k[:, :, lanes].reshape(tokens, HD), v[:, :, lanes].reshape(tokens, HD)
        k_far = halo[h, :, :PAIR * TILE].reshape(KINDS * PAIR * TILE, HD)
        v_far = halo[h, :, PAIR * TILE:].reshape(KINDS * PAIR * TILE, HD)
        qt = q[span, lanes]
        shift = bias[pl.ds(first // TILE, block // TILE)]

        def masked(s, shift):
            return (s.reshape(block // TILE, TILE, -1) * scale + shift).reshape(block, -1)

        s_own = masked(dot(qt, k_own, 1), shift[:, :, :near])
        s_far = masked(dot(qt, k_far, 1), shift[:, :, near:])
        top = jnp.maximum(jnp.max(s_own, axis=1, keepdims=True), jnp.max(s_far, axis=1, keepdims=True))
        p_own, p_far = jnp.exp2(s_own - top), jnp.exp2(s_far - top)
        total = jnp.sum(p_own, axis=1, keepdims=True) + jnp.sum(p_far, axis=1, keepdims=True)
        summed = dot(p_own.astype(jnp.bfloat16), v_own, 0) + dot(p_far.astype(jnp.bfloat16), v_far, 0)
        ctx[span, lanes] = (summed * (1.0 / total)).astype(ctx.dtype)

    def halves(whole):
        low, high = whole[:rows], whole[rows:]
        return jnp.where(parity == 0, low, high), jnp.where(parity == 0, high, low)

    def sum_copy(step, c):
        return pltpu.make_async_remote_copy(
            src_ref=sum_out.at[step - 1, c], dst_ref=sum_in.at[step - 1, c],
            send_sem=sum_send.at[step - 1, c], recv_sem=sum_recv.at[step - 1, c],
            device_id=(device, mate), device_id_type=MESH)

    def part_copy(step, c):
        return pltpu.make_async_remote_copy(
            src_ref=part_out.at[step - 1, c], dst_ref=part_in.at[step - 1, c],
            send_sem=part_send.at[step - 1, c], recv_sem=part_recv.at[step - 1, c],
            device_id=(device, peer(step)), device_id_type=MESH)

    def own_copy(c):
        return pltpu.make_async_remote_copy(
            src_ref=own_out.at[c], dst_ref=own_in.at[c],
            send_sem=own_send.at[c], recv_sem=own_recv.at[c],
            device_id=(device, mate), device_id_type=MESH)

    def ctx_copy(j):
        lanes = pl.ds(pl.multiple_of((first_late + j) * HD, HD), HD)
        return pltpu.make_async_remote_copy(
            src_ref=ctx.at[pl.ds(block_start(1), block), lanes],
            dst_ref=ctx_far.at[:, pl.ds(pl.multiple_of(j * HD, HD), HD)],
            send_sem=ctx_send.at[j], recv_sem=ctx_recv.at[j],
            device_id=(device, peer(1)), device_id_type=MESH)

    stages = [(count, [(step, c) for step in range(1, pairs) for c in range(chunks) if late[c] == count])
              for count in sorted(set(late), reverse=True)]

    held = stages[-1][1][-HOLD:] if most_late and HOLD else []

    def project(count, ready):
        depth = (heads - count) * HD
        for step, c in ready:
            whole = dot(ctx[pl.ds(block_start(step), block), :depth], w[:depth, c * chunk:(c + 1) * chunk], 0)
            mine, other = halves(whole)
            kept[step - 1, c] = mine
            sum_out[step - 1, c] = other.astype(sum_out.dtype)
            sum_copy(step, c).start()

    def forward(ready):
        for step, c in ready:
            sum_copy(step, c).wait_recv()
            part_out[step - 1, c] = (kept[step - 1, c] + sum_in[step - 1, c].astype(jnp.float32)).astype(part_out.dtype)
            part_copy(step, c).start()

    def arrive(n, h):
        direct_copy(h, n).wait_recv()
        if n:
            pass_copy(h, n).wait_recv()

    pass_on(0)

    def one_head(h, carry):
        @pl.when(h + ahead + lead < heads)
        def _():
            send_turn(h + ahead + lead)

        @pl.when(h + ahead < heads)
        def _():
            send_rest(h + ahead)
        for kind in range(KINDS):
            if kind == near_kind:
                by_count(inside(sources[kind]), turned_source, lambda n: arrive(n, h))
                continue

            @pl.when(inside(sources[kind]))
            def _(kind=kind):
                halo_copy(h, kind).wait_recv()
        lanes = pl.ds(pl.multiple_of(h * HD, HD), HD)
        for step in range(1, pairs):
            attend(h, lanes, block_start(step))
        if most_late:
            @pl.when(h >= first_late)
            def _():
                ctx_copy(h - first_late).start()
        for count, ready in stages:
            @pl.when(h == heads - 1 - count)
            def _(count=count, ready=ready):
                project(count, ready)

        @pl.when(h + 1 < heads)
        def _():
            pass_on(h + 1)

        for count, ready in stages:
            @pl.when(h == heads - 1 - count)
            def _(ready=ready):
                forward([x for x in ready if x not in held])
        if held:
            @pl.when(h == heads - 1)
            def _():
                forward(held)
        attend(h, lanes, block_start(0))
        return carry

    lax.fori_loop(0, heads, one_head, 0)

    mine_rows = pl.ds(block_start(0), block)
    for c in range(chunks):
        own[c] = dot(ctx[mine_rows, :], w[:, c * chunk:(c + 1) * chunk], 0)
    for c in late_chunks:
        w_copy(c).wait_recv()
    for j in range(most_late):
        ctx_copy(j).wait_recv()
    for c in range(chunks):
        whole = own[c]
        if late[c]:
            skip = (most_late - late[c]) * HD
            whole = whole + dot(ctx_far[:, skip:], w_far[c, skip:, :], 0)
        mine, other = halves(whole)
        own[c, :rows] = mine
        own_out[c] = other.astype(own_out.dtype)
        own_copy(c).start()
    def left(n, h):
        direct_copy(h, n).wait_send()
        if n:
            turn_copy(h, n).wait_send()

    def drain_halo(h, carry):
        by_count(inside(hop), turned_passing, lambda n: pass_copy(h, n).wait_send() if n else None)
        for kind in range(KINDS):
            if kind == near_kind:
                by_count(inside(readers[kind]), turned_mine, lambda n: left(n, h))
                continue

            @pl.when(inside(readers[kind]))
            def _(kind=kind):
                halo_copy(h, kind).wait_send()
        return carry
    lax.fori_loop(0, heads, drain_halo, 0)
    for c in late_chunks:
        w_copy(c).wait_send()
    for j in range(most_late):
        ctx_copy(j).wait_send()
    for c in range(chunks):
        own_copy(c).wait_send()
        for step in range(1, pairs):
            sum_copy(step, c).wait_send()
    for _, ready in stages:
        for c in [c for step, c in ready if step == 1]:
            own_copy(c).wait_recv()
            total = own[c, :rows] + own_in[c].astype(jnp.float32)
            for step in range(1, pairs):
                part_copy(step, c).wait_recv()
                total = total + part_in[step - 1, c].astype(jnp.float32)
            out[:, c * chunk:(c + 1) * chunk] = total.astype(out.dtype)

    for c in range(chunks):
        for step in range(1, pairs):
            part_copy(step, c).wait_send()


def lateness(heads, pairs, chunks):
    if pairs != 2 or heads < 3:
        return (0,) * chunks
    return (2,2,1,1,1,1)


def body(queries, keys, values, kv_tiles, out_weight):
    tokens, columns = queries.shape
    width = out_weight.shape[1]
    devices, groups = lax.axis_size("ctx"), lax.axis_size("head")
    heads, rows, pairs = columns // HD, tokens // groups, groups // 2
    chunk = min(width, 512)
    chunks = width // chunk
    late = lateness(heads, pairs, chunks)
    deep = max(max(late), 1)
    sems = pltpu.SemaphoreType.DMA
    bf16, f32 = jnp.bfloat16, jnp.float32
    operands = (kv_tiles.T, queries, keys.reshape(-1, TILE, columns), values.reshape(-1, TILE, columns), out_weight)
    return pl.pallas_call(
        functools.partial(kernel, devices, groups, chunk, late),
        out_shape=jax.ShapeDtypeStruct((rows, width), bf16),
        in_specs=[pl.BlockSpec(memory_space=pltpu.HBM)] * len(operands),
        out_specs=pl.BlockSpec(memory_space=pltpu.VMEM),
        scratch_shapes=[
            pltpu.SMEM(kv_tiles.shape[::-1], jnp.int32),
            pltpu.VMEM((tokens, columns), bf16),
            pltpu.VMEM((tokens // TILE, TILE, columns), bf16),
            pltpu.VMEM((tokens // TILE, TILE, columns), bf16),
            pltpu.VMEM((columns, width), bf16),
            pltpu.VMEM((tokens // TILE, 1, tokens + KINDS * PAIR * TILE), f32),
            pltpu.VMEM((heads, KINDS, 2 * PAIR * TILE, HD), bf16),
            pltpu.VMEM((heads, KINDS, 2 * PAIR * TILE, HD), bf16),
            pltpu.VMEM((heads, 2 * PAIR * TILE, HD), bf16),
            pltpu.VMEM((tokens, columns), bf16),
            pltpu.VMEM((2 * rows, deep * HD), bf16),
            pltpu.VMEM((chunks, deep * HD, chunk), bf16),
            pltpu.VMEM((pairs - 1, chunks, rows, chunk), f32),
            pltpu.VMEM((pairs - 1, chunks, rows, chunk), bf16),
            pltpu.VMEM((pairs - 1, chunks, rows, chunk), bf16),
            pltpu.VMEM((pairs - 1, chunks, rows, chunk), bf16),
            pltpu.VMEM((pairs - 1, chunks, rows, chunk), bf16),
            pltpu.VMEM((chunks, 2 * rows, chunk), f32),
            pltpu.VMEM((chunks, rows, chunk), bf16),
            pltpu.VMEM((chunks, rows, chunk), bf16),
            sems((5,)),
            sems((heads, KINDS)), sems((heads, KINDS)),
            sems((heads,)), sems((heads,)), sems((heads,)), sems((heads,)),
            sems((chunks,)), sems((chunks,)),
            sems((deep,)), sems((deep,)),
            sems((pairs - 1, chunks)), sems((pairs - 1, chunks)),
            sems((pairs - 1, chunks)), sems((pairs - 1, chunks)),
            sems((chunks,)), sems((chunks,)),
        ],
        compiler_params=pltpu.CompilerParams(
            collective_id=0, has_side_effects=True, vmem_limit_bytes=40 * 2 ** 20),
    )(*[pltpu.with_memory_space_constraint(operand, pltpu.HBM) for operand in operands])


def solution(mesh):
    return jax.shard_map(
        body,
        mesh=mesh,
        in_specs=(P("ctx", "head"), P("ctx", "head"), P("ctx", "head"), P(), P("head", None)),
        out_specs=P(("ctx", "head"), None),
        check_vma=False,
    )
```

```python
import functools
import math

import jax
import jax.numpy as jnp
from jax import lax
from jax.experimental import pallas as pl
from jax.experimental.pallas import tpu as pltpu
from jax.sharding import PartitionSpec as P

HD = 128
TILE = 128
REACH = 2
PAIR = 2
KINDS = 2 * REACH
MASKED = -1e30
HOLD = 2
QUARTERS = 4
MESH = pl.DeviceIdType.MESH


def dot(a, b, contract):
    return lax.dot_general(a, b, (((1,), (contract,)), ((), ())), preferred_element_type=jnp.float32)


def kernel(devices, groups, chunk, late, lists_in, q_in, k_in, v_in, w_in, out,
           lists, q, k, v, w, bias, packed, halo, passing, ctx, ctx_far, w_far,
           ctx_swap, w_swap, kept, sum_out, sum_in, part_out, part_in, own, own_out, own_in,
           load_sems, halo_send, halo_recv, turn_send, turn_recv, pass_send, pass_recv, w_send, w_recv, ctx_send, ctx_recv,
           ctx_swap_send, ctx_swap_recv, w_swap_send, w_swap_recv, sum_send, sum_recv, part_send, part_recv, own_send, own_recv):
    device, group = lax.axis_index("ctx"), lax.axis_index("head")
    parity, place = group % 2, group // 2
    mate = group + 1 - 2 * parity
    tokens, columns = q.shape
    heads, tiles = columns // HD, tokens // TILE
    width = out.shape[1]
    rows = tokens // groups
    block = 2 * rows
    pairs = groups // 2
    chunks = width // chunk
    most_late = max(late)
    first_late = heads - most_late

    counts = sorted(set(late), reverse=True)
    stages = [[(step, c) for step in range(1, pairs) for c in range(chunks) if late[c] == count] for count in counts]

    side = device % 2
    sources = (device + 1 - 2 * side, device - 1 + 2 * side, device - 2, device + 2)
    readers = (sources[0], sources[1], device + 2, device - 2)

    near_kind = 1
    quarter = 2 * PAIR * TILE // QUARTERS
    layers, layer = devices // 2, device // 2
    hop = device + 2 - 4 * side

    def inside(index):
        return (index >= 0) & (index < devices)

    def turned(side, layer):
        return jnp.where(side == 1, layers - 1 - layer, layer) * QUARTERS // layers

    turned_mine, turned_passing = turned(side, layer), turned(1 - side, layer)
    turned_source = turned(1 - side, layer - 1 + 2 * side)

    def by_count(condition, count, act):
        for n in range(QUARTERS):
            @pl.when(condition & (count == n))
            def _(n=n):
                act(n)

    def peer(step):
        return 2 * ((place + step) % pairs) + parity

    load_lists = pltpu.make_async_copy(lists_in, lists, load_sems.at[0])
    load_k = pltpu.make_async_copy(k_in, k, load_sems.at[1])
    load_v = pltpu.make_async_copy(v_in, v, load_sems.at[2])
    load_q = pltpu.make_async_copy(q_in, q, load_sems.at[3])
    load_w = pltpu.make_async_copy(w_in, w, load_sems.at[4])
    for load in (load_lists, load_k, load_v, load_q, load_w):
        load.start()

    barrier = pltpu.get_barrier_semaphore()
    expected = jnp.int32(pairs)
    for kind in range(KINDS):
        @pl.when(inside(readers[kind]))
        def _(kind=kind):
            pl.semaphore_signal(barrier, 1, device_id=(readers[kind], group), device_id_type=MESH)
        expected = expected + inside(sources[kind]).astype(jnp.int32)
    pl.semaphore_signal(barrier, 1, device_id=(device, mate), device_id_type=MESH)
    for step in range(1, pairs):
        pl.semaphore_signal(barrier, 1, device_id=(device, peer(step)), device_id_type=MESH)

    load_lists.wait()
    entries = lists.shape[0]

    def sent(r, found):
        found = list(found)
        for kind in range(KINDS):
            row = (readers[kind] + devices) % devices * tiles + r
            for e in range(entries):
                x = lists[e, row] - device * tiles
                least, most = found[2 * kind], found[2 * kind + 1]
                found[2 * kind] = jnp.minimum(least, jnp.where(x < 0, tiles - 1, x))
                found[2 * kind + 1] = jnp.maximum(most, jnp.where(x >= tiles, 0, x))
        return tuple(found)

    ids = lax.fori_loop(0, tiles, sent, (jnp.int32(tiles - 1), jnp.int32(0)) * KINDS)

    load_k.wait()
    load_v.wait()
    pl.semaphore_wait(barrier, expected)

    def w_copy(c):
        source = w_in.at[pl.ds((heads - late[c]) * HD, late[c] * HD), pl.ds(c * chunk, chunk)]
        return pltpu.make_async_remote_copy(
            src_ref=source, dst_ref=w_far.at[c, pl.ds((most_late - late[c]) * HD, late[c] * HD)],
            send_sem=w_send.at[c], recv_sem=w_recv.at[c],
            device_id=(device, peer(1)), device_id_type=MESH)

    late_chunks = [c for c in range(chunks) if late[c]]
    for c in late_chunks:
        w_copy(c).start()

    def halo_copy(h, kind):
        return pltpu.make_async_remote_copy(
            src_ref=packed.at[h, kind], dst_ref=halo.at[h, kind],
            send_sem=halo_send.at[h, kind], recv_sem=halo_recv.at[h, kind],
            device_id=(readers[kind], group), device_id_type=MESH)

    def direct_copy(h, n):
        span = pl.ds(n * quarter, (QUARTERS - n) * quarter)
        return pltpu.make_async_remote_copy(
            src_ref=packed.at[h, near_kind, span], dst_ref=halo.at[h, near_kind, span],
            send_sem=halo_send.at[h, near_kind], recv_sem=halo_recv.at[h, near_kind],
            device_id=(readers[near_kind], group), device_id_type=MESH)

    def turn_copy(h, n):
        span = pl.ds(0, n * quarter)
        return pltpu.make_async_remote_copy(
            src_ref=packed.at[h, near_kind, span], dst_ref=passing.at[h, span],
            send_sem=turn_send.at[h], recv_sem=turn_recv.at[h],
            device_id=(readers[0], group), device_id_type=MESH)

    def pass_copy(h, n):
        span = pl.ds(0, n * quarter)
        return pltpu.make_async_remote_copy(
            src_ref=passing.at[h, span], dst_ref=halo.at[h, near_kind, span],
            send_sem=pass_send.at[h], recv_sem=pass_recv.at[h],
            device_id=(hop, group), device_id_type=MESH)

    def pass_on(h):
        def one(n):
            if n:
                turn_copy(h, n).wait_recv()
                pass_copy(h, n).start()
        by_count(inside(hop), turned_passing, one)

    def pack(h, kinds):
        lanes = pl.ds(pl.multiple_of(h * HD, HD), HD)
        for kind in kinds:
            for which in range(PAIR):
                picked = ids[PAIR * kind + which]
                for part, ref in ((0, k), (1, v)):
                    at = (part * PAIR + which) * TILE
                    packed[h, kind, at:at + TILE, :] = ref[picked, :, lanes]

    def send_turn(h):
        pack(h, (near_kind,))
        by_count(inside(readers[near_kind]), turned_mine, lambda n: turn_copy(h, n).start() if n else None)

    def send_rest(h):
        pack(h, [kind for kind in range(KINDS) if kind != near_kind])
        for kind in (3, near_kind, 0, 2):
            if kind == near_kind:
                by_count(inside(readers[kind]), turned_mine, lambda n: direct_copy(h, n).start())
                continue

            @pl.when(inside(readers[kind]))
            def _(kind=kind):
                halo_copy(h, kind).start()

    send_turn(0)
    send_rest(0)

    def w_swap_copy(stage):
        columns_of = [c for step, c in stages[stage] if step == 1]
        lanes = pl.ds(columns_of[0] * chunk, len(columns_of) * chunk)
        return pltpu.make_async_remote_copy(
            src_ref=w_in.at[pl.ds((heads - 1 - counts[stage]) * HD, HD), lanes], dst_ref=w_swap.at[:, lanes],
            send_sem=w_swap_send.at[stage], recv_sem=w_swap_recv.at[stage],
            device_id=(device, mate), device_id_type=MESH)

    for stage in range(len(stages)):
        w_swap_copy(stage).start()

    for kind in range(KINDS):
        @pl.when(jnp.logical_not(inside(sources[kind])))
        def _(kind=kind):
            halo[:, kind] = jnp.zeros((heads,) + halo.shape[2:], halo.dtype)

    def received(r, found):
        found = list(found)
        for e in range(entries):
            tile = lists[e, device * tiles + r]
            for kind in range(KINDS):
                x = tile - sources[kind] * tiles
                least, most = found[2 * kind], found[2 * kind + 1]
                found[2 * kind] = jnp.minimum(least, jnp.where(x < 0, tiles, x))
                found[2 * kind + 1] = jnp.maximum(most, jnp.where(x >= tiles, -1, x))
        return tuple(found)

    found = lax.fori_loop(0, tiles, received, (jnp.int32(tiles), jnp.int32(-1)) * KINDS)
    listed = [device * tiles + j for j in range(tiles)]
    for kind in range(KINDS):
        least, most = found[2 * kind], found[2 * kind + 1]
        listed.append(jnp.where(least < tiles, sources[kind] * tiles + least, -1))
        listed.append(jnp.where(most > least, sources[kind] * tiles + most, -1))

    def mask(t, carry):
        added = [jnp.float32(MASKED)] * len(listed)
        for e in range(entries):
            tile = lists[e, device * tiles + t]
            added = [jnp.where(tile == other, 0.0, value) for other, value in zip(listed, added)]
        for j, value in enumerate(added):
            bias[t, :, j * TILE:(j + 1) * TILE] = jnp.full((1, TILE), value, jnp.float32)
        return carry

    lax.fori_loop(0, tiles, mask, 0)
    load_q.wait()
    load_w.wait()
    for stage in range(len(stages)):
        w_swap_copy(stage).wait_recv()

    scale = HD ** -0.5 * math.log2(math.e)
    near = tokens

    def block_start(step):
        return pl.multiple_of((place + step) % pairs * block, block)

    def attend(h, lanes, first):
        span = pl.ds(pl.multiple_of(first, TILE), block)
        k_own, v_own = k[:, :, lanes].reshape(tokens, HD), v[:, :, lanes].reshape(tokens, HD)
        k_far = halo[h, :, :PAIR * TILE].reshape(KINDS * PAIR * TILE, HD)
        v_far = halo[h, :, PAIR * TILE:].reshape(KINDS * PAIR * TILE, HD)
        qt = q[span, lanes]
        shift = bias[pl.ds(first // TILE, block // TILE)]

        def masked(s, shift):
            return (s.reshape(block // TILE, TILE, -1) * scale + shift).reshape(block, -1)

        s_own = masked(dot(qt, k_own, 1), shift[:, :, :near])
        s_far = masked(dot(qt, k_far, 1), shift[:, :, near:])
        top = jnp.maximum(jnp.max(s_own, axis=1, keepdims=True), jnp.max(s_far, axis=1, keepdims=True))
        p_own, p_far = jnp.exp2(s_own - top), jnp.exp2(s_far - top)
        total = jnp.sum(p_own, axis=1, keepdims=True) + jnp.sum(p_far, axis=1, keepdims=True)
        summed = dot(p_own.astype(jnp.bfloat16), v_own, 0) + dot(p_far.astype(jnp.bfloat16), v_far, 0)
        ctx[span, lanes] = (summed * (1.0 / total)).astype(ctx.dtype)

    def halves(whole):
        low, high = whole[:rows], whole[rows:]
        return jnp.where(parity == 0, low, high), jnp.where(parity == 0, high, low)

    def sum_copy(step, c):
        return pltpu.make_async_remote_copy(
            src_ref=sum_out.at[step - 1, c], dst_ref=sum_in.at[step - 1, c],
            send_sem=sum_send.at[step - 1, c], recv_sem=sum_recv.at[step - 1, c],
            device_id=(device, mate), device_id_type=MESH)

    def part_copy(step, c):
        return pltpu.make_async_remote_copy(
            src_ref=part_out.at[step - 1, c], dst_ref=part_in.at[step - 1, c],
            send_sem=part_send.at[step - 1, c], recv_sem=part_recv.at[step - 1, c],
            device_id=(device, peer(step)), device_id_type=MESH)

    def own_copy(c):
        return pltpu.make_async_remote_copy(
            src_ref=own_out.at[c], dst_ref=own_in.at[c],
            send_sem=own_send.at[c], recv_sem=own_recv.at[c],
            device_id=(device, mate), device_id_type=MESH)

    def ctx_copy(j):
        lanes = pl.ds(pl.multiple_of((first_late + j) * HD, HD), HD)
        return pltpu.make_async_remote_copy(
            src_ref=ctx.at[pl.ds(block_start(1), block), lanes],
            dst_ref=ctx_far.at[:, pl.ds(pl.multiple_of(j * HD, HD), HD)],
            send_sem=ctx_send.at[j], recv_sem=ctx_recv.at[j],
            device_id=(device, peer(1)), device_id_type=MESH)

    held = stages[-1][-HOLD:] if most_late else []

    def rows_of(step, of_mate):
        which = 1 - parity if of_mate else parity
        return pl.ds(pl.multiple_of(block_start(step) + which * rows, rows), rows)

    def ctx_swap_copy(stage, step):
        last = heads - 1 - counts[stage]
        return pltpu.make_async_remote_copy(
            src_ref=ctx.at[rows_of(step, True), pl.ds(last * HD, HD)], dst_ref=ctx_swap.at[stage, step - 1],
            send_sem=ctx_swap_send.at[stage, step - 1], recv_sem=ctx_swap_recv.at[stage, step - 1],
            device_id=(device, mate), device_id_type=MESH)

    def project(stage):
        depth = (heads - 1 - counts[stage]) * HD
        for step, c in stages[stage]:
            whole = dot(ctx[pl.ds(block_start(step), block), :depth], w[:depth, c * chunk:(c + 1) * chunk], 0)
            mine, other = halves(whole)
            kept[step - 1, c] = mine
            sum_out[step - 1, c] = other.astype(sum_out.dtype)
            sum_copy(step, c).start()

    def add_last(stage):
        last = pl.ds((heads - 1 - counts[stage]) * HD, HD)
        for step, c in stages[stage]:
            kept[step - 1, c] += dot(ctx[rows_of(step, False), last], w[last, c * chunk:(c + 1) * chunk], 0)
        for step in range(1, pairs):
            ctx_swap_copy(stage, step).wait_recv()

    def forward(stage, ready):
        for step, c in ready:
            total = kept[step - 1, c] + dot(ctx_swap[stage, step - 1], w_swap[:, c * chunk:(c + 1) * chunk], 0)
            sum_copy(step, c).wait_recv()
            part_out[step - 1, c] = (total + sum_in[step - 1, c].astype(jnp.float32)).astype(part_out.dtype)
            part_copy(step, c).start()

    def arrive(n, h):
        direct_copy(h, n).wait_recv()
        if n:
            pass_copy(h, n).wait_recv()

    pass_on(0)

    def one_head(h, carry):
        @pl.when(h + 1 < heads)
        def _():
            send_turn(h + 1)
            send_rest(h + 1)
        for kind in range(KINDS):
            if kind == near_kind:
                by_count(inside(sources[kind]), turned_source, lambda n: arrive(n, h))
                continue

            @pl.when(inside(sources[kind]))
            def _(kind=kind):
                halo_copy(h, kind).wait_recv()
        lanes = pl.ds(pl.multiple_of(h * HD, HD), HD)
        for step in range(1, pairs):
            attend(h, lanes, block_start(step))
        for stage, count in enumerate(counts):
            @pl.when(h == heads - 1 - count)
            def _(stage=stage):
                for step in range(1, pairs):
                    ctx_swap_copy(stage, step).start()
        if most_late:
            @pl.when(h >= first_late)
            def _():
                ctx_copy(h - first_late).start()
        for stage, count in enumerate(counts):
            @pl.when(h == heads - 1 - count)
            def _(stage=stage):
                add_last(stage)
                forward(stage, [x for x in stages[stage] if x not in held])
        if held:
            @pl.when(h == heads - 1)
            def _():
                forward(len(stages) - 1, held)

        @pl.when(h + 1 < heads)
        def _():
            pass_on(h + 1)

        attend(h, lanes, block_start(0))
        for stage, count in enumerate(counts):
            @pl.when(h == heads - 2 - count)
            def _(stage=stage):
                project(stage)
        return carry

    lax.fori_loop(0, heads, one_head, 0)

    mine_rows = pl.ds(block_start(0), block)
    for c in range(chunks):
        own[c] = dot(ctx[mine_rows, :], w[:, c * chunk:(c + 1) * chunk], 0)
    for c in late_chunks:
        w_copy(c).wait_recv()
    for j in range(most_late):
        ctx_copy(j).wait_recv()
    for c in range(chunks):
        whole = own[c]
        if late[c]:
            skip = (most_late - late[c]) * HD
            whole = whole + dot(ctx_far[:, skip:], w_far[c, skip:, :], 0)
        mine, other = halves(whole)
        own[c, :rows] = mine
        own_out[c] = other.astype(own_out.dtype)
        own_copy(c).start()
    def left(n, h):
        direct_copy(h, n).wait_send()
        if n:
            turn_copy(h, n).wait_send()

    def drain_halo(h, carry):
        by_count(inside(hop), turned_passing, lambda n: pass_copy(h, n).wait_send() if n else None)
        for kind in range(KINDS):
            if kind == near_kind:
                by_count(inside(readers[kind]), turned_mine, lambda n: left(n, h))
                continue

            @pl.when(inside(readers[kind]))
            def _(kind=kind):
                halo_copy(h, kind).wait_send()
        return carry
    lax.fori_loop(0, heads, drain_halo, 0)
    for c in late_chunks:
        w_copy(c).wait_send()
    for stage in range(len(stages)):
        w_swap_copy(stage).wait_send()
        for step in range(1, pairs):
            ctx_swap_copy(stage, step).wait_send()
    for j in range(most_late):
        ctx_copy(j).wait_send()
    for c in range(chunks):
        own_copy(c).wait_send()
        for step in range(1, pairs):
            sum_copy(step, c).wait_send()
    for ready in stages:
        for c in [c for step, c in ready if step == 1]:
            own_copy(c).wait_recv()
            total = own[c, :rows] + own_in[c].astype(jnp.float32)
            for step in range(1, pairs):
                part_copy(step, c).wait_recv()
                total = total + part_in[step - 1, c].astype(jnp.float32)
            out[:, c * chunk:(c + 1) * chunk] = total.astype(out.dtype)

    for c in range(chunks):
        for step in range(1, pairs):
            part_copy(step, c).wait_send()


def lateness(heads, pairs, chunks):
    if pairs != 2 or heads < 3:
        return (0,) * chunks
    return tuple(2 if 3 * c < chunks else 1 for c in range(chunks))


def body(queries, keys, values, kv_tiles, out_weight):
    tokens, columns = queries.shape
    width = out_weight.shape[1]
    devices, groups = lax.axis_size("ctx"), lax.axis_size("head")
    heads, rows, pairs = columns // HD, tokens // groups, groups // 2
    chunk = min(width, 512)
    chunks = width // chunk
    late = lateness(heads, pairs, chunks)
    deep = max(max(late), 1)
    sems = pltpu.SemaphoreType.DMA
    bf16, f32 = jnp.bfloat16, jnp.float32
    operands = (kv_tiles.T, queries, keys.reshape(-1, TILE, columns), values.reshape(-1, TILE, columns), out_weight)
    return pl.pallas_call(
        functools.partial(kernel, devices, groups, chunk, late),
        out_shape=jax.ShapeDtypeStruct((rows, width), bf16),
        in_specs=[pl.BlockSpec(memory_space=pltpu.HBM)] * len(operands),
        out_specs=pl.BlockSpec(memory_space=pltpu.VMEM),
        scratch_shapes=[
            pltpu.SMEM(kv_tiles.shape[::-1], jnp.int32),
            pltpu.VMEM((tokens, columns), bf16),
            pltpu.VMEM((tokens // TILE, TILE, columns), bf16),
            pltpu.VMEM((tokens // TILE, TILE, columns), bf16),
            pltpu.VMEM((columns, width), bf16),
            pltpu.VMEM((tokens // TILE, 1, tokens + KINDS * PAIR * TILE), f32),
            pltpu.VMEM((heads, KINDS, 2 * PAIR * TILE, HD), bf16),
            pltpu.VMEM((heads, KINDS, 2 * PAIR * TILE, HD), bf16),
            pltpu.VMEM((heads, 2 * PAIR * TILE, HD), bf16),
            pltpu.VMEM((tokens, columns), bf16),
            pltpu.VMEM((2 * rows, deep * HD), bf16),
            pltpu.VMEM((chunks, deep * HD, chunk), bf16),
            pltpu.VMEM((len(set(late)), pairs - 1, rows, HD), bf16),
            pltpu.VMEM((HD, width), bf16),
            pltpu.VMEM((pairs - 1, chunks, rows, chunk), f32),
            pltpu.VMEM((pairs - 1, chunks, rows, chunk), bf16),
            pltpu.VMEM((pairs - 1, chunks, rows, chunk), bf16),
            pltpu.VMEM((pairs - 1, chunks, rows, chunk), bf16),
            pltpu.VMEM((pairs - 1, chunks, rows, chunk), bf16),
            pltpu.VMEM((chunks, 2 * rows, chunk), f32),
            pltpu.VMEM((chunks, rows, chunk), bf16),
            pltpu.VMEM((chunks, rows, chunk), bf16),
            sems((5,)),
            sems((heads, KINDS)), sems((heads, KINDS)),
            sems((heads,)), sems((heads,)), sems((heads,)), sems((heads,)),
            sems((chunks,)), sems((chunks,)),
            sems((deep,)), sems((deep,)),
            sems((len(set(late)), pairs - 1)), sems((len(set(late)), pairs - 1)),
            sems((len(set(late)),)), sems((len(set(late)),)),
            sems((pairs - 1, chunks)), sems((pairs - 1, chunks)),
            sems((pairs - 1, chunks)), sems((pairs - 1, chunks)),
            sems((chunks,)), sems((chunks,)),
        ],
        compiler_params=pltpu.CompilerParams(
            collective_id=0, has_side_effects=True, vmem_limit_bytes=40 * 2 ** 20),
    )(*[pltpu.with_memory_space_constraint(operand, pltpu.HBM) for operand in operands])


def solution(mesh):
    return jax.shard_map(
        body,
        mesh=mesh,
        in_specs=(P("ctx", "head"), P("ctx", "head"), P("ctx", "head"), P(), P("head", None)),
        out_specs=P(("ctx", "head"), None),
        check_vma=False,
    )
```

```python
import functools
import math

import jax
import jax.numpy as jnp
from jax import lax
from jax.experimental import pallas as pl
from jax.experimental.pallas import tpu as pltpu
from jax.sharding import PartitionSpec as P

HD = 128
TILE = 128
REACH = 2
PAIR = 2
KINDS = 2 * REACH
MASKED = -1e30
HOLD = 2
QUARTERS = 4
MESH = pl.DeviceIdType.MESH


def dot(a, b, contract):
    return lax.dot_general(a, b, (((1,), (contract,)), ((), ())), preferred_element_type=jnp.float32)


def kernel(devices, groups, chunk, late, lists_in, q_in, k_in, v_in, w_in, out,
           lists, q, k, v, w, bias, packed, halo, passing, ctx, ctx_far, w_far,
           ctx_swap, w_swap, kept, sum_out, sum_in, part_out, part_in, own, own_out, own_in,
           load_sems, halo_send, halo_recv, turn_send, turn_recv, pass_send, pass_recv, w_send, w_recv, ctx_send, ctx_recv,
           ctx_swap_send, ctx_swap_recv, w_swap_send, w_swap_recv, sum_send, sum_recv, part_send, part_recv, own_send, own_recv):
    device, group = lax.axis_index("ctx"), lax.axis_index("head")
    parity, place = group % 2, group // 2
    mate = group + 1 - 2 * parity
    tokens, columns = q.shape
    heads, tiles = columns // HD, tokens // TILE
    width = out.shape[1]
    rows = tokens // groups
    block = 2 * rows
    pairs = groups // 2
    chunks = width // chunk
    most_late = max(late)
    first_late = heads - most_late

    counts = sorted(set(late), reverse=True)
    stages = [[(step, c) for step in range(1, pairs) for c in range(chunks) if late[c] == count] for count in counts]

    side = device % 2
    sources = (device + 1 - 2 * side, device - 1 + 2 * side, device - 2, device + 2)
    readers = (sources[0], sources[1], device + 2, device - 2)

    near_kind = 1
    quarter = 2 * PAIR * TILE // QUARTERS
    layers, layer = devices // 2, device // 2
    hop = device + 2 - 4 * side

    def inside(index):
        return (index >= 0) & (index < devices)

    def turned(side, layer):
        return jnp.where(side == 1, layers - 1 - layer, layer) * QUARTERS // layers

    turned_mine, turned_passing = turned(side, layer), turned(1 - side, layer)
    turned_source = turned(1 - side, layer - 1 + 2 * side)

    def by_count(condition, count, act):
        for n in range(QUARTERS):
            @pl.when(condition & (count == n))
            def _(n=n):
                act(n)

    def peer(step):
        return 2 * ((place + step) % pairs) + parity

    load_lists = pltpu.make_async_copy(lists_in, lists, load_sems.at[0])
    load_k = pltpu.make_async_copy(k_in, k, load_sems.at[1])
    load_v = pltpu.make_async_copy(v_in, v, load_sems.at[2])
    load_q = pltpu.make_async_copy(q_in, q, load_sems.at[3])
    load_w = pltpu.make_async_copy(w_in, w, load_sems.at[4])
    for load in (load_lists, load_k, load_v, load_q, load_w):
        load.start()

    barrier = pltpu.get_barrier_semaphore()
    expected = jnp.int32(pairs)
    for kind in range(KINDS):
        @pl.when(inside(readers[kind]))
        def _(kind=kind):
            pl.semaphore_signal(barrier, 1, device_id=(readers[kind], group), device_id_type=MESH)
        expected = expected + inside(sources[kind]).astype(jnp.int32)
    pl.semaphore_signal(barrier, 1, device_id=(device, mate), device_id_type=MESH)
    for step in range(1, pairs):
        pl.semaphore_signal(barrier, 1, device_id=(device, peer(step)), device_id_type=MESH)

    load_lists.wait()
    entries = lists.shape[0]

    def sent(r, found):
        found = list(found)
        for kind in range(KINDS):
            row = (readers[kind] + devices) % devices * tiles + r
            for e in range(entries):
                x = lists[e, row] - device * tiles
                least, most = found[2 * kind], found[2 * kind + 1]
                found[2 * kind] = jnp.minimum(least, jnp.where(x < 0, tiles - 1, x))
                found[2 * kind + 1] = jnp.maximum(most, jnp.where(x >= tiles, 0, x))
        return tuple(found)

    ids = lax.fori_loop(0, tiles, sent, (jnp.int32(tiles - 1), jnp.int32(0)) * KINDS)

    load_k.wait()
    load_v.wait()
    pl.semaphore_wait(barrier, expected)

    def w_copy(c):
        source = w_in.at[pl.ds((heads - late[c]) * HD, late[c] * HD), pl.ds(c * chunk, chunk)]
        return pltpu.make_async_remote_copy(
            src_ref=source, dst_ref=w_far.at[c, pl.ds((most_late - late[c]) * HD, late[c] * HD)],
            send_sem=w_send.at[c], recv_sem=w_recv.at[c],
            device_id=(device, peer(1)), device_id_type=MESH)

    late_chunks = [c for c in range(chunks) if late[c]]
    for c in late_chunks:
        w_copy(c).start()

    def halo_copy(h, kind):
        return pltpu.make_async_remote_copy(
            src_ref=packed.at[h, kind], dst_ref=halo.at[h, kind],
            send_sem=halo_send.at[h, kind], recv_sem=halo_recv.at[h, kind],
            device_id=(readers[kind], group), device_id_type=MESH)

    def direct_copy(h, n):
        span = pl.ds(n * quarter, (QUARTERS - n) * quarter)
        return pltpu.make_async_remote_copy(
            src_ref=packed.at[h, near_kind, span], dst_ref=halo.at[h, near_kind, span],
            send_sem=halo_send.at[h, near_kind], recv_sem=halo_recv.at[h, near_kind],
            device_id=(readers[near_kind], group), device_id_type=MESH)

    def turn_copy(h, n):
        span = pl.ds(0, n * quarter)
        return pltpu.make_async_remote_copy(
            src_ref=packed.at[h, near_kind, span], dst_ref=passing.at[h, span],
            send_sem=turn_send.at[h], recv_sem=turn_recv.at[h],
            device_id=(readers[0], group), device_id_type=MESH)

    def pass_copy(h, n):
        span = pl.ds(0, n * quarter)
        return pltpu.make_async_remote_copy(
            src_ref=passing.at[h, span], dst_ref=halo.at[h, near_kind, span],
            send_sem=pass_send.at[h], recv_sem=pass_recv.at[h],
            device_id=(hop, group), device_id_type=MESH)

    def pass_on(h):
        def one(n):
            if n:
                turn_copy(h, n).wait_recv()
                pass_copy(h, n).start()
        by_count(inside(hop), turned_passing, one)

    def pack(h, kinds):
        lanes = pl.ds(pl.multiple_of(h * HD, HD), HD)
        for kind in kinds:
            for which in range(PAIR):
                picked = ids[PAIR * kind + which]
                for part, ref in ((0, k), (1, v)):
                    at = (part * PAIR + which) * TILE
                    packed[h, kind, at:at + TILE, :] = ref[picked, :, lanes]

    def send_turn(h):
        pack(h, (near_kind,))
        by_count(inside(readers[near_kind]), turned_mine, lambda n: turn_copy(h, n).start() if n else None)

    def send_rest(h):
        pack(h, [kind for kind in range(KINDS) if kind != near_kind])
        for kind in (3, near_kind, 0, 2):
            if kind == near_kind:
                by_count(inside(readers[kind]), turned_mine, lambda n: direct_copy(h, n).start())
                continue

            @pl.when(inside(readers[kind]))
            def _(kind=kind):
                halo_copy(h, kind).start()

    send_turn(0)
    send_rest(0)

    def w_swap_copy(stage):
        columns_of = [c for step, c in stages[stage] if step == 1]
        lanes = pl.ds(columns_of[0] * chunk, len(columns_of) * chunk)
        return pltpu.make_async_remote_copy(
            src_ref=w_in.at[pl.ds((heads - 1 - counts[stage]) * HD, HD), lanes], dst_ref=w_swap.at[:, lanes],
            send_sem=w_swap_send.at[stage], recv_sem=w_swap_recv.at[stage],
            device_id=(device, mate), device_id_type=MESH)

    for stage in range(len(stages)):
        w_swap_copy(stage).start()

    for kind in range(KINDS):
        @pl.when(jnp.logical_not(inside(sources[kind])))
        def _(kind=kind):
            halo[:, kind] = jnp.zeros((heads,) + halo.shape[2:], halo.dtype)

    def received(r, found):
        found = list(found)
        for e in range(entries):
            tile = lists[e, device * tiles + r]
            for kind in range(KINDS):
                x = tile - sources[kind] * tiles
                least, most = found[2 * kind], found[2 * kind + 1]
                found[2 * kind] = jnp.minimum(least, jnp.where(x < 0, tiles, x))
                found[2 * kind + 1] = jnp.maximum(most, jnp.where(x >= tiles, -1, x))
        return tuple(found)

    found = lax.fori_loop(0, tiles, received, (jnp.int32(tiles), jnp.int32(-1)) * KINDS)
    listed = [device * tiles + j for j in range(tiles)]
    for kind in range(KINDS):
        least, most = found[2 * kind], found[2 * kind + 1]
        listed.append(jnp.where(least < tiles, sources[kind] * tiles + least, -1))
        listed.append(jnp.where(most > least, sources[kind] * tiles + most, -1))

    def mask(t, carry):
        added = [jnp.float32(MASKED)] * len(listed)
        for e in range(entries):
            tile = lists[e, device * tiles + t]
            added = [jnp.where(tile == other, 0.0, value) for other, value in zip(listed, added)]
        for j, value in enumerate(added):
            bias[t, :, j * TILE:(j + 1) * TILE] = jnp.full((1, TILE), value, jnp.float32)
        return carry

    lax.fori_loop(0, tiles, mask, 0)
    load_q.wait()
    load_w.wait()
    for stage in range(len(stages)):
        w_swap_copy(stage).wait_recv()

    scale = HD ** -0.5 * math.log2(math.e)
    near = tokens

    def block_start(step):
        return pl.multiple_of((place + step) % pairs * block, block)

    def attend(h, lanes, first):
        span = pl.ds(pl.multiple_of(first, TILE), block)
        k_own, v_own = k[:, :, lanes].reshape(tokens, HD), v[:, :, lanes].reshape(tokens, HD)
        k_far = halo[h, :, :PAIR * TILE].reshape(KINDS * PAIR * TILE, HD)
        v_far = halo[h, :, PAIR * TILE:].reshape(KINDS * PAIR * TILE, HD)
        qt = q[span, lanes]
        shift = bias[pl.ds(first // TILE, block // TILE)]

        def masked(s, shift):
            return (s.reshape(block // TILE, TILE, -1) * scale + shift).reshape(block, -1)

        s_own = masked(dot(qt, k_own, 1), shift[:, :, :near])
        s_far = masked(dot(qt, k_far, 1), shift[:, :, near:])
        top = jnp.maximum(jnp.max(s_own, axis=1, keepdims=True), jnp.max(s_far, axis=1, keepdims=True))
        p_own, p_far = jnp.exp2(s_own - top), jnp.exp2(s_far - top)
        total = jnp.sum(p_own, axis=1, keepdims=True) + jnp.sum(p_far, axis=1, keepdims=True)
        summed = dot(p_own.astype(jnp.bfloat16), v_own, 0) + dot(p_far.astype(jnp.bfloat16), v_far, 0)
        ctx[span, lanes] = (summed * (1.0 / total)).astype(ctx.dtype)

    def scores(h, lanes, first, columns, keys):
        qt = q[pl.ds(pl.multiple_of(first, TILE), block), lanes]
        shift = bias[pl.ds(first // TILE, block // TILE)][:, :, columns]
        return (dot(qt, keys, 1).reshape(block // TILE, TILE, -1) * scale + shift).reshape(block, -1)

    def attend_own(h, lanes, first):
        s = scores(h, lanes, first, slice(0, near), k[:, :, lanes].reshape(tokens, HD))
        top = jnp.max(s, axis=1, keepdims=True)
        p = jnp.exp2(s - top)
        return top, jnp.sum(p, axis=1, keepdims=True), dot(p.astype(jnp.bfloat16), v[:, :, lanes].reshape(tokens, HD), 0)

    def attend_more(h, lanes, first, state, kinds):
        top, total, summed = state
        low, high = kinds[0], kinds[-1] + 1
        columns = slice(near + low * PAIR * TILE, near + high * PAIR * TILE)
        s = scores(h, lanes, first, columns, halo[h, low:high, :PAIR * TILE].reshape(-1, HD))
        most = jnp.maximum(top, jnp.max(s, axis=1, keepdims=True))
        p, less = jnp.exp2(s - most), jnp.exp2(top - most)
        far = dot(p.astype(jnp.bfloat16), halo[h, low:high, PAIR * TILE:].reshape(-1, HD), 0)
        return most, total * less + jnp.sum(p, axis=1, keepdims=True), summed * less + far

    def halves(whole):
        low, high = whole[:rows], whole[rows:]
        return jnp.where(parity == 0, low, high), jnp.where(parity == 0, high, low)

    def sum_copy(step, c):
        return pltpu.make_async_remote_copy(
            src_ref=sum_out.at[step - 1, c], dst_ref=sum_in.at[step - 1, c],
            send_sem=sum_send.at[step - 1, c], recv_sem=sum_recv.at[step - 1, c],
            device_id=(device, mate), device_id_type=MESH)

    def part_copy(step, c):
        return pltpu.make_async_remote_copy(
            src_ref=part_out.at[step - 1, c], dst_ref=part_in.at[step - 1, c],
            send_sem=part_send.at[step - 1, c], recv_sem=part_recv.at[step - 1, c],
            device_id=(device, peer(step)), device_id_type=MESH)

    def own_copy(c):
        return pltpu.make_async_remote_copy(
            src_ref=own_out.at[c], dst_ref=own_in.at[c],
            send_sem=own_send.at[c], recv_sem=own_recv.at[c],
            device_id=(device, mate), device_id_type=MESH)

    def ctx_copy(j):
        lanes = pl.ds(pl.multiple_of((first_late + j) * HD, HD), HD)
        return pltpu.make_async_remote_copy(
            src_ref=ctx.at[pl.ds(block_start(1), block), lanes],
            dst_ref=ctx_far.at[:, pl.ds(pl.multiple_of(j * HD, HD), HD)],
            send_sem=ctx_send.at[j], recv_sem=ctx_recv.at[j],
            device_id=(device, peer(1)), device_id_type=MESH)

    held = stages[-1][-HOLD:] if most_late else []

    def rows_of(step, of_mate):
        which = 1 - parity if of_mate else parity
        return pl.ds(pl.multiple_of(block_start(step) + which * rows, rows), rows)

    def ctx_swap_copy(stage, step):
        last = heads - 1 - counts[stage]
        return pltpu.make_async_remote_copy(
            src_ref=ctx.at[rows_of(step, True), pl.ds(last * HD, HD)], dst_ref=ctx_swap.at[stage, step - 1],
            send_sem=ctx_swap_send.at[stage, step - 1], recv_sem=ctx_swap_recv.at[stage, step - 1],
            device_id=(device, mate), device_id_type=MESH)

    def project(stage):
        depth = (heads - 1 - counts[stage]) * HD
        for step, c in stages[stage]:
            whole = dot(ctx[pl.ds(block_start(step), block), :depth], w[:depth, c * chunk:(c + 1) * chunk], 0)
            mine, other = halves(whole)
            kept[step - 1, c] = mine
            sum_out[step - 1, c] = other.astype(sum_out.dtype)
            sum_copy(step, c).start()

    def add_last(stage):
        last = pl.ds((heads - 1 - counts[stage]) * HD, HD)
        for step, c in stages[stage]:
            kept[step - 1, c] += dot(ctx[rows_of(step, False), last], w[last, c * chunk:(c + 1) * chunk], 0)
        for step in range(1, pairs):
            ctx_swap_copy(stage, step).wait_recv()

    def forward(stage, ready):
        for step, c in ready:
            total = kept[step - 1, c] + dot(ctx_swap[stage, step - 1], w_swap[:, c * chunk:(c + 1) * chunk], 0)
            sum_copy(step, c).wait_recv()
            part_out[step - 1, c] = (total + sum_in[step - 1, c].astype(jnp.float32)).astype(part_out.dtype)
            part_copy(step, c).start()

    def arrive(n, h):
        direct_copy(h, n).wait_recv()
        if n:
            pass_copy(h, n).wait_recv()

    pass_on(0)

    def one_head(h, carry):
        @pl.when(h + 1 < heads)
        def _():
            send_turn(h + 1)
            send_rest(h + 1)
        lanes = pl.ds(pl.multiple_of(h * HD, HD), HD)
        firsts = [block_start(step) for step in range(1, pairs)]
        states = [attend_own(h, lanes, first) for first in firsts]
        for kinds in ((2, 3), (0, 1)):
            for kind in kinds:
                if kind == near_kind:
                    by_count(inside(sources[kind]), turned_source, lambda n: arrive(n, h))
                    continue

                @pl.when(inside(sources[kind]))
                def _(kind=kind):
                    halo_copy(h, kind).wait_recv()
            states = [attend_more(h, lanes, first, state, kinds) for first, state in zip(firsts, states)]
        for first, (_, total, summed) in zip(firsts, states):
            ctx[pl.ds(pl.multiple_of(first, TILE), block), lanes] = (summed * (1.0 / total)).astype(ctx.dtype)
        for stage, count in enumerate(counts):
            @pl.when(h == heads - 1 - count)
            def _(stage=stage):
                for step in range(1, pairs):
                    ctx_swap_copy(stage, step).start()
        if most_late:
            @pl.when(h >= first_late)
            def _():
                ctx_copy(h - first_late).start()
        for stage, count in enumerate(counts):
            @pl.when(h == heads - 1 - count)
            def _(stage=stage):
                add_last(stage)
                forward(stage, [x for x in stages[stage] if x not in held])
        if held:
            @pl.when(h == heads - 1)
            def _():
                forward(len(stages) - 1, held)

        @pl.when(h + 1 < heads)
        def _():
            pass_on(h + 1)

        attend(h, lanes, block_start(0))
        for stage, count in enumerate(counts):
            @pl.when(h == heads - 2 - count)
            def _(stage=stage):
                project(stage)
        return carry

    lax.fori_loop(0, heads, one_head, 0)

    mine_rows = pl.ds(block_start(0), block)
    for c in range(chunks):
        own[c] = dot(ctx[mine_rows, :], w[:, c * chunk:(c + 1) * chunk], 0)
    for c in late_chunks:
        w_copy(c).wait_recv()
    for j in range(most_late):
        ctx_copy(j).wait_recv()
    for c in range(chunks):
        whole = own[c]
        if late[c]:
            skip = (most_late - late[c]) * HD
            whole = whole + dot(ctx_far[:, skip:], w_far[c, skip:, :], 0)
        mine, other = halves(whole)
        own[c, :rows] = mine
        own_out[c] = other.astype(own_out.dtype)
        own_copy(c).start()
    def left(n, h):
        direct_copy(h, n).wait_send()
        if n:
            turn_copy(h, n).wait_send()

    def drain_halo(h, carry):
        by_count(inside(hop), turned_passing, lambda n: pass_copy(h, n).wait_send() if n else None)
        for kind in range(KINDS):
            if kind == near_kind:
                by_count(inside(readers[kind]), turned_mine, lambda n: left(n, h))
                continue

            @pl.when(inside(readers[kind]))
            def _(kind=kind):
                halo_copy(h, kind).wait_send()
        return carry
    lax.fori_loop(0, heads, drain_halo, 0)
    for c in late_chunks:
        w_copy(c).wait_send()
    for stage in range(len(stages)):
        w_swap_copy(stage).wait_send()
        for step in range(1, pairs):
            ctx_swap_copy(stage, step).wait_send()
    for j in range(most_late):
        ctx_copy(j).wait_send()
    for c in range(chunks):
        own_copy(c).wait_send()
        for step in range(1, pairs):
            sum_copy(step, c).wait_send()
    for ready in stages:
        for c in [c for step, c in ready if step == 1]:
            own_copy(c).wait_recv()
            total = own[c, :rows] + own_in[c].astype(jnp.float32)
            for step in range(1, pairs):
                part_copy(step, c).wait_recv()
                total = total + part_in[step - 1, c].astype(jnp.float32)
            out[:, c * chunk:(c + 1) * chunk] = total.astype(out.dtype)

    for c in range(chunks):
        for step in range(1, pairs):
            part_copy(step, c).wait_send()


def lateness(heads, pairs, chunks):
    if pairs != 2 or heads < 3:
        return (0,) * chunks
    return tuple(2 if 3 * c < chunks else 1 for c in range(chunks))


def body(queries, keys, values, kv_tiles, out_weight):
    tokens, columns = queries.shape
    width = out_weight.shape[1]
    devices, groups = lax.axis_size("ctx"), lax.axis_size("head")
    heads, rows, pairs = columns // HD, tokens // groups, groups // 2
    chunk = min(width, 512)
    chunks = width // chunk
    late = lateness(heads, pairs, chunks)
    deep = max(max(late), 1)
    sems = pltpu.SemaphoreType.DMA
    bf16, f32 = jnp.bfloat16, jnp.float32
    operands = (kv_tiles.T, queries, keys.reshape(-1, TILE, columns), values.reshape(-1, TILE, columns), out_weight)
    return pl.pallas_call(
        functools.partial(kernel, devices, groups, chunk, late),
        out_shape=jax.ShapeDtypeStruct((rows, width), bf16),
        in_specs=[pl.BlockSpec(memory_space=pltpu.HBM)] * len(operands),
        out_specs=pl.BlockSpec(memory_space=pltpu.VMEM),
        scratch_shapes=[
            pltpu.SMEM(kv_tiles.shape[::-1], jnp.int32),
            pltpu.VMEM((tokens, columns), bf16),
            pltpu.VMEM((tokens // TILE, TILE, columns), bf16),
            pltpu.VMEM((tokens // TILE, TILE, columns), bf16),
            pltpu.VMEM((columns, width), bf16),
            pltpu.VMEM((tokens // TILE, 1, tokens + KINDS * PAIR * TILE), f32),
            pltpu.VMEM((heads, KINDS, 2 * PAIR * TILE, HD), bf16),
            pltpu.VMEM((heads, KINDS, 2 * PAIR * TILE, HD), bf16),
            pltpu.VMEM((heads, 2 * PAIR * TILE, HD), bf16),
            pltpu.VMEM((tokens, columns), bf16),
            pltpu.VMEM((2 * rows, deep * HD), bf16),
            pltpu.VMEM((chunks, deep * HD, chunk), bf16),
            pltpu.VMEM((len(set(late)), pairs - 1, rows, HD), bf16),
            pltpu.VMEM((HD, width), bf16),
            pltpu.VMEM((pairs - 1, chunks, rows, chunk), f32),
            pltpu.VMEM((pairs - 1, chunks, rows, chunk), bf16),
            pltpu.VMEM((pairs - 1, chunks, rows, chunk), bf16),
            pltpu.VMEM((pairs - 1, chunks, rows, chunk), bf16),
            pltpu.VMEM((pairs - 1, chunks, rows, chunk), bf16),
            pltpu.VMEM((chunks, 2 * rows, chunk), f32),
            pltpu.VMEM((chunks, rows, chunk), bf16),
            pltpu.VMEM((chunks, rows, chunk), bf16),
            sems((5,)),
            sems((heads, KINDS)), sems((heads, KINDS)),
            sems((heads,)), sems((heads,)), sems((heads,)), sems((heads,)),
            sems((chunks,)), sems((chunks,)),
            sems((deep,)), sems((deep,)),
            sems((len(set(late)), pairs - 1)), sems((len(set(late)), pairs - 1)),
            sems((len(set(late)),)), sems((len(set(late)),)),
            sems((pairs - 1, chunks)), sems((pairs - 1, chunks)),
            sems((pairs - 1, chunks)), sems((pairs - 1, chunks)),
            sems((chunks,)), sems((chunks,)),
        ],
        compiler_params=pltpu.CompilerParams(
            collective_id=0, has_side_effects=True, vmem_limit_bytes=40 * 2 ** 20),
    )(*[pltpu.with_memory_space_constraint(operand, pltpu.HBM) for operand in operands])


def solution(mesh):
    return jax.shard_map(
        body,
        mesh=mesh,
        in_specs=(P("ctx", "head"), P("ctx", "head"), P("ctx", "head"), P(), P("head", None)),
        out_specs=P(("ctx", "head"), None),
        check_vma=False,
    )
```

```python
import functools
import math

import jax
import jax.numpy as jnp
from jax import lax
from jax.experimental import pallas as pl
from jax.experimental.pallas import tpu as pltpu
from jax.sharding import PartitionSpec as P

HD = 128
TILE = 128
REACH = 2
PAIR = 2
KINDS = 2 * REACH
MASKED = -1e30
HOLD = 2
QUARTERS = 4
MESH = pl.DeviceIdType.MESH


def dot(a, b, contract):
    return lax.dot_general(a, b, (((1,), (contract,)), ((), ())), preferred_element_type=jnp.float32)


def kernel(devices, groups, chunk, late, lists_in, q_in, k_in, v_in, w_in, out,
           lists, q, k, v, w, bias, packed, halo, passing, ctx, ctx_far, w_far,
           ctx_swap, w_swap, kept, sum_out, sum_in, part_out, part_in, own, own_out, own_in,
           load_sems, halo_send, halo_recv, turn_send, turn_recv, pass_send, pass_recv, w_send, w_recv, ctx_send, ctx_recv,
           ctx_swap_send, ctx_swap_recv, w_swap_send, w_swap_recv, sum_send, sum_recv, part_send, part_recv, own_send, own_recv):
    device, group = lax.axis_index("ctx"), lax.axis_index("head")
    parity, place = group % 2, group // 2
    mate = group + 1 - 2 * parity
    tokens, columns = q.shape
    heads, tiles = columns // HD, tokens // TILE
    width = out.shape[1]
    rows = tokens // groups
    block = 2 * rows
    pairs = groups // 2
    chunks = width // chunk
    most_late = max(late)
    first_late = heads - most_late

    counts = sorted(set(late), reverse=True)
    stages = [[(step, c) for step in range(1, pairs) for c in range(chunks) if late[c] == count] for count in counts]

    side = device % 2
    sources = (device + 1 - 2 * side, device - 1 + 2 * side, device - 2, device + 2)
    readers = (sources[0], sources[1], device + 2, device - 2)

    near_kind = 1
    quarter = 2 * PAIR * TILE // QUARTERS
    layers, layer = devices // 2, device // 2
    hop = device + 2 - 4 * side

    def inside(index):
        return (index >= 0) & (index < devices)

    def turned(side, layer):
        return jnp.where(side == 1, layers - 1 - layer, layer) * QUARTERS // layers

    turned_mine, turned_passing = turned(side, layer), turned(1 - side, layer)
    turned_source = turned(1 - side, layer - 1 + 2 * side)

    def by_count(condition, count, act):
        for n in range(QUARTERS):
            @pl.when(condition & (count == n))
            def _(n=n):
                act(n)

    def peer(step):
        return 2 * ((place + step) % pairs) + parity

    load_lists = pltpu.make_async_copy(lists_in, lists, load_sems.at[0])
    load_k = pltpu.make_async_copy(k_in, k, load_sems.at[1])
    load_v = pltpu.make_async_copy(v_in, v, load_sems.at[2])
    load_q = pltpu.make_async_copy(q_in, q, load_sems.at[3])
    load_w = pltpu.make_async_copy(w_in, w, load_sems.at[4])
    for load in (load_lists, load_k, load_v, load_q, load_w):
        load.start()

    barrier = pltpu.get_barrier_semaphore()
    expected = jnp.int32(pairs)
    for kind in range(KINDS):
        @pl.when(inside(readers[kind]))
        def _(kind=kind):
            pl.semaphore_signal(barrier, 1, device_id=(readers[kind], group), device_id_type=MESH)
        expected = expected + inside(sources[kind]).astype(jnp.int32)
    pl.semaphore_signal(barrier, 1, device_id=(device, mate), device_id_type=MESH)
    for step in range(1, pairs):
        pl.semaphore_signal(barrier, 1, device_id=(device, peer(step)), device_id_type=MESH)

    load_lists.wait()
    entries = lists.shape[0]

    def sent(r, found):
        found = list(found)
        for kind in range(KINDS):
            row = (readers[kind] + devices) % devices * tiles + r
            for e in range(entries):
                x = lists[e, row] - device * tiles
                least, most = found[2 * kind], found[2 * kind + 1]
                found[2 * kind] = jnp.minimum(least, jnp.where(x < 0, tiles - 1, x))
                found[2 * kind + 1] = jnp.maximum(most, jnp.where(x >= tiles, 0, x))
        return tuple(found)

    ids = lax.fori_loop(0, tiles, sent, (jnp.int32(tiles - 1), jnp.int32(0)) * KINDS)

    load_k.wait()
    load_v.wait()
    pl.semaphore_wait(barrier, expected)

    def w_copy(c):
        source = w_in.at[pl.ds((heads - late[c]) * HD, late[c] * HD), pl.ds(c * chunk, chunk)]
        return pltpu.make_async_remote_copy(
            src_ref=source, dst_ref=w_far.at[c, pl.ds((most_late - late[c]) * HD, late[c] * HD)],
            send_sem=w_send.at[c], recv_sem=w_recv.at[c],
            device_id=(device, peer(1)), device_id_type=MESH)

    late_chunks = [c for c in range(chunks) if late[c]]
    for c in late_chunks:
        w_copy(c).start()

    def halo_copy(h, kind):
        return pltpu.make_async_remote_copy(
            src_ref=packed.at[h, kind], dst_ref=halo.at[h, kind],
            send_sem=halo_send.at[h, kind], recv_sem=halo_recv.at[h, kind],
            device_id=(readers[kind], group), device_id_type=MESH)

    def direct_copy(h, n):
        span = pl.ds(n * quarter, (QUARTERS - n) * quarter)
        return pltpu.make_async_remote_copy(
            src_ref=packed.at[h, near_kind, span], dst_ref=halo.at[h, near_kind, span],
            send_sem=halo_send.at[h, near_kind], recv_sem=halo_recv.at[h, near_kind],
            device_id=(readers[near_kind], group), device_id_type=MESH)

    def turn_copy(h, n):
        span = pl.ds(0, n * quarter)
        return pltpu.make_async_remote_copy(
            src_ref=packed.at[h, near_kind, span], dst_ref=passing.at[h, span],
            send_sem=turn_send.at[h], recv_sem=turn_recv.at[h],
            device_id=(readers[0], group), device_id_type=MESH)

    def pass_copy(h, n):
        span = pl.ds(0, n * quarter)
        return pltpu.make_async_remote_copy(
            src_ref=passing.at[h, span], dst_ref=halo.at[h, near_kind, span],
            send_sem=pass_send.at[h], recv_sem=pass_recv.at[h],
            device_id=(hop, group), device_id_type=MESH)

    def pass_on(h):
        def one(n):
            if n:
                turn_copy(h, n).wait_recv()
                pass_copy(h, n).start()
        by_count(inside(hop), turned_passing, one)

    def pack(h, kinds):
        lanes = pl.ds(pl.multiple_of(h * HD, HD), HD)
        for kind in kinds:
            for which in range(PAIR):
                picked = ids[PAIR * kind + which]
                for part, ref in ((0, k), (1, v)):
                    at = (part * PAIR + which) * TILE
                    packed[h, kind, at:at + TILE, :] = ref[picked, :, lanes]

    def send_turn(h):
        pack(h, (near_kind,))
        by_count(inside(readers[near_kind]), turned_mine, lambda n: turn_copy(h, n).start() if n else None)

    def send_rest(h):
        pack(h, [kind for kind in range(KINDS) if kind != near_kind])
        for kind in (3, near_kind, 0, 2):
            if kind == near_kind:
                by_count(inside(readers[kind]), turned_mine, lambda n: direct_copy(h, n).start())
                continue

            @pl.when(inside(readers[kind]))
            def _(kind=kind):
                halo_copy(h, kind).start()

    send_turn(0)
    send_rest(0)

    def w_swap_copy(stage):
        columns_of = [c for step, c in stages[stage] if step == 1]
        lanes = pl.ds(columns_of[0] * chunk, len(columns_of) * chunk)
        return pltpu.make_async_remote_copy(
            src_ref=w_in.at[pl.ds((heads - 1 - counts[stage]) * HD, HD), lanes], dst_ref=w_swap.at[:, lanes],
            send_sem=w_swap_send.at[stage], recv_sem=w_swap_recv.at[stage],
            device_id=(device, mate), device_id_type=MESH)

    for stage in range(len(stages)):
        w_swap_copy(stage).start()

    for kind in range(KINDS):
        @pl.when(jnp.logical_not(inside(sources[kind])))
        def _(kind=kind):
            halo[:, kind] = jnp.zeros((heads,) + halo.shape[2:], halo.dtype)

    def received(r, found):
        found = list(found)
        for e in range(entries):
            tile = lists[e, device * tiles + r]
            for kind in range(KINDS):
                x = tile - sources[kind] * tiles
                least, most = found[2 * kind], found[2 * kind + 1]
                found[2 * kind] = jnp.minimum(least, jnp.where(x < 0, tiles, x))
                found[2 * kind + 1] = jnp.maximum(most, jnp.where(x >= tiles, -1, x))
        return tuple(found)

    found = lax.fori_loop(0, tiles, received, (jnp.int32(tiles), jnp.int32(-1)) * KINDS)
    listed = [device * tiles + j for j in range(tiles)]
    for kind in range(KINDS):
        least, most = found[2 * kind], found[2 * kind + 1]
        listed.append(jnp.where(least < tiles, sources[kind] * tiles + least, -1))
        listed.append(jnp.where(most > least, sources[kind] * tiles + most, -1))

    def mask(t, carry):
        added = [jnp.float32(MASKED)] * len(listed)
        for e in range(entries):
            tile = lists[e, device * tiles + t]
            added = [jnp.where(tile == other, 0.0, value) for other, value in zip(listed, added)]
        for j, value in enumerate(added):
            bias[t, :, j * TILE:(j + 1) * TILE] = jnp.full((1, TILE), value, jnp.float32)
        return carry

    lax.fori_loop(0, tiles, mask, 0)
    load_q.wait()
    load_w.wait()
    for stage in range(len(stages)):
        w_swap_copy(stage).wait_recv()

    scale = HD ** -0.5 * math.log2(math.e)
    near = tokens

    def block_start(step):
        return pl.multiple_of((place + step) % pairs * block, block)

    def attend(h, lanes, first):
        span = pl.ds(pl.multiple_of(first, TILE), block)
        k_own, v_own = k[:, :, lanes].reshape(tokens, HD), v[:, :, lanes].reshape(tokens, HD)
        k_far = halo[h, :, :PAIR * TILE].reshape(KINDS * PAIR * TILE, HD)
        v_far = halo[h, :, PAIR * TILE:].reshape(KINDS * PAIR * TILE, HD)
        qt = q[span, lanes]
        shift = bias[pl.ds(first // TILE, block // TILE)]

        def masked(s, shift):
            return (s.reshape(block // TILE, TILE, -1) * scale + shift).reshape(block, -1)

        s_own = masked(dot(qt, k_own, 1), shift[:, :, :near])
        s_far = masked(dot(qt, k_far, 1), shift[:, :, near:])
        top = jnp.maximum(jnp.max(s_own, axis=1, keepdims=True), jnp.max(s_far, axis=1, keepdims=True))
        p_own, p_far = jnp.exp2(s_own - top), jnp.exp2(s_far - top)
        total = jnp.sum(p_own, axis=1, keepdims=True) + jnp.sum(p_far, axis=1, keepdims=True)
        summed = dot(p_own.astype(jnp.bfloat16), v_own, 0) + dot(p_far.astype(jnp.bfloat16), v_far, 0)
        ctx[span, lanes] = (summed * (1.0 / total)).astype(ctx.dtype)

    def scores(h, lanes, first, columns, keys):
        qt = q[pl.ds(pl.multiple_of(first, TILE), block), lanes]
        shift = bias[pl.ds(first // TILE, block // TILE)][:, :, columns]
        return (dot(qt, keys, 1).reshape(block // TILE, TILE, -1) * scale + shift).reshape(block, -1)

    def attend_own(h, lanes, first):
        s = scores(h, lanes, first, slice(0, near), k[:, :, lanes].reshape(tokens, HD))
        top = jnp.max(s, axis=1, keepdims=True)
        p = jnp.exp2(s - top)
        return top, jnp.sum(p, axis=1, keepdims=True), dot(p.astype(jnp.bfloat16), v[:, :, lanes].reshape(tokens, HD), 0)

    def attend_more(h, lanes, first, state, kinds):
        top, total, summed = state
        low, high = kinds[0], kinds[-1] + 1
        columns = slice(near + low * PAIR * TILE, near + high * PAIR * TILE)
        s = scores(h, lanes, first, columns, halo[h, low:high, :PAIR * TILE].reshape(-1, HD))
        most = jnp.maximum(top, jnp.max(s, axis=1, keepdims=True))
        p, less = jnp.exp2(s - most), jnp.exp2(top - most)
        far = dot(p.astype(jnp.bfloat16), halo[h, low:high, PAIR * TILE:].reshape(-1, HD), 0)
        return most, total * less + jnp.sum(p, axis=1, keepdims=True), summed * less + far

    def halves(whole):
        low, high = whole[:rows], whole[rows:]
        return jnp.where(parity == 0, low, high), jnp.where(parity == 0, high, low)

    def sum_copy(step, c):
        return pltpu.make_async_remote_copy(
            src_ref=sum_out.at[step - 1, c], dst_ref=sum_in.at[step - 1, c],
            send_sem=sum_send.at[step - 1, c], recv_sem=sum_recv.at[step - 1, c],
            device_id=(device, mate), device_id_type=MESH)

    def part_copy(step, c):
        return pltpu.make_async_remote_copy(
            src_ref=part_out.at[step - 1, c], dst_ref=part_in.at[step - 1, c],
            send_sem=part_send.at[step - 1, c], recv_sem=part_recv.at[step - 1, c],
            device_id=(device, peer(step)), device_id_type=MESH)

    def own_copy(c):
        return pltpu.make_async_remote_copy(
            src_ref=own_out.at[c], dst_ref=own_in.at[c],
            send_sem=own_send.at[c], recv_sem=own_recv.at[c],
            device_id=(device, mate), device_id_type=MESH)

    def ctx_copy(j):
        lanes = pl.ds(pl.multiple_of((first_late + j) * HD, HD), HD)
        return pltpu.make_async_remote_copy(
            src_ref=ctx.at[pl.ds(block_start(1), block), lanes],
            dst_ref=ctx_far.at[:, pl.ds(pl.multiple_of(j * HD, HD), HD)],
            send_sem=ctx_send.at[j], recv_sem=ctx_recv.at[j],
            device_id=(device, peer(1)), device_id_type=MESH)

    held = stages[-1][-HOLD:] if most_late else []

    def rows_of(step, of_mate):
        which = 1 - parity if of_mate else parity
        return pl.ds(pl.multiple_of(block_start(step) + which * rows, rows), rows)

    def ctx_swap_copy(stage, step):
        last = heads - 1 - counts[stage]
        return pltpu.make_async_remote_copy(
            src_ref=ctx.at[rows_of(step, True), pl.ds(last * HD, HD)], dst_ref=ctx_swap.at[stage, step - 1],
            send_sem=ctx_swap_send.at[stage, step - 1], recv_sem=ctx_swap_recv.at[stage, step - 1],
            device_id=(device, mate), device_id_type=MESH)

    def project(stage):
        depth = (heads - 1 - counts[stage]) * HD
        for step, c in stages[stage]:
            whole = dot(ctx[pl.ds(block_start(step), block), :depth], w[:depth, c * chunk:(c + 1) * chunk], 0)
            mine, other = halves(whole)
            kept[step - 1, c] = mine
            sum_out[step - 1, c] = other.astype(sum_out.dtype)
            sum_copy(step, c).start()

    def add_last(stage):
        last = pl.ds((heads - 1 - counts[stage]) * HD, HD)
        for step, c in stages[stage]:
            kept[step - 1, c] += dot(ctx[rows_of(step, False), last], w[last, c * chunk:(c + 1) * chunk], 0)
        for step in range(1, pairs):
            ctx_swap_copy(stage, step).wait_recv()

    def forward(stage, ready):
        for step, c in ready:
            total = kept[step - 1, c] + dot(ctx_swap[stage, step - 1], w_swap[:, c * chunk:(c + 1) * chunk], 0)
            sum_copy(step, c).wait_recv()
            part_out[step - 1, c] = (total + sum_in[step - 1, c].astype(jnp.float32)).astype(part_out.dtype)
            part_copy(step, c).start()

    def arrive(n, h):
        direct_copy(h, n).wait_recv()
        if n:
            pass_copy(h, n).wait_recv()

    pass_on(0)

    def one_head(h, carry):
        @pl.when(h + 1 < heads)
        def _():
            send_turn(h + 1)
            send_rest(h + 1)
        lanes = pl.ds(pl.multiple_of(h * HD, HD), HD)
        firsts = [block_start(step) for step in range(1, pairs)]
        states = [attend_own(h, lanes, first) for first in firsts]
        for kinds in ((2, 3), (0, 1)):
            for kind in kinds:
                if kind == near_kind:
                    by_count(inside(sources[kind]), turned_source, lambda n: arrive(n, h))
                    continue

                @pl.when(inside(sources[kind]))
                def _(kind=kind):
                    halo_copy(h, kind).wait_recv()
            states = [attend_more(h, lanes, first, state, kinds) for first, state in zip(firsts, states)]
        for first, (_, total, summed) in zip(firsts, states):
            ctx[pl.ds(pl.multiple_of(first, TILE), block), lanes] = (summed * (1.0 / total)).astype(ctx.dtype)
        for stage, count in enumerate(counts):
            @pl.when(h == heads - 1 - count)
            def _(stage=stage):
                for step in range(1, pairs):
                    ctx_swap_copy(stage, step).start()
        if most_late:
            @pl.when(h >= first_late)
            def _():
                ctx_copy(h - first_late).start()
        @pl.when((h + 1 < heads) & (h < heads - 1 - counts[0]))
        def _():
            pass_on(h + 1)

        attend(h, lanes, block_start(0))
        for stage, count in enumerate(counts):
            @pl.when(h == heads - 1 - count)
            def _(stage=stage):
                add_last(stage)
                forward(stage, [x for x in stages[stage] if x not in held])
        if held:
            @pl.when(h == heads - 1)
            def _():
                forward(len(stages) - 1, held)

        @pl.when((h + 1 < heads) & (h >= heads - 1 - counts[0]))
        def _():
            pass_on(h + 1)

        for stage, count in enumerate(counts):
            @pl.when(h == heads - 2 - count)
            def _(stage=stage):
                project(stage)
        return carry

    lax.fori_loop(0, heads, one_head, 0)

    mine_rows = pl.ds(block_start(0), block)
    for c in range(chunks):
        own[c] = dot(ctx[mine_rows, :], w[:, c * chunk:(c + 1) * chunk], 0)
    for c in late_chunks:
        w_copy(c).wait_recv()
    for j in range(most_late):
        ctx_copy(j).wait_recv()
    for c in range(chunks):
        whole = own[c]
        if late[c]:
            skip = (most_late - late[c]) * HD
            whole = whole + dot(ctx_far[:, skip:], w_far[c, skip:, :], 0)
        mine, other = halves(whole)
        own[c, :rows] = mine
        own_out[c] = other.astype(own_out.dtype)
        own_copy(c).start()
    def left(n, h):
        direct_copy(h, n).wait_send()
        if n:
            turn_copy(h, n).wait_send()

    def drain_halo(h, carry):
        by_count(inside(hop), turned_passing, lambda n: pass_copy(h, n).wait_send() if n else None)
        for kind in range(KINDS):
            if kind == near_kind:
                by_count(inside(readers[kind]), turned_mine, lambda n: left(n, h))
                continue

            @pl.when(inside(readers[kind]))
            def _(kind=kind):
                halo_copy(h, kind).wait_send()
        return carry
    lax.fori_loop(0, heads, drain_halo, 0)
    for c in late_chunks:
        w_copy(c).wait_send()
    for stage in range(len(stages)):
        w_swap_copy(stage).wait_send()
        for step in range(1, pairs):
            ctx_swap_copy(stage, step).wait_send()
    for j in range(most_late):
        ctx_copy(j).wait_send()
    for c in range(chunks):
        own_copy(c).wait_send()
        for step in range(1, pairs):
            sum_copy(step, c).wait_send()
    for ready in stages:
        for c in [c for step, c in ready if step == 1]:
            own_copy(c).wait_recv()
            total = own[c, :rows] + own_in[c].astype(jnp.float32)
            for step in range(1, pairs):
                part_copy(step, c).wait_recv()
                total = total + part_in[step - 1, c].astype(jnp.float32)
            out[:, c * chunk:(c + 1) * chunk] = total.astype(out.dtype)

    for c in range(chunks):
        for step in range(1, pairs):
            part_copy(step, c).wait_send()


def lateness(heads, pairs, chunks):
    if pairs != 2 or heads < 3:
        return (0,) * chunks
    return tuple(2 if 3 * c < chunks else 1 for c in range(chunks))


def body(queries, keys, values, kv_tiles, out_weight):
    tokens, columns = queries.shape
    width = out_weight.shape[1]
    devices, groups = lax.axis_size("ctx"), lax.axis_size("head")
    heads, rows, pairs = columns // HD, tokens // groups, groups // 2
    chunk = min(width, 512)
    chunks = width // chunk
    late = lateness(heads, pairs, chunks)
    deep = max(max(late), 1)
    sems = pltpu.SemaphoreType.DMA
    bf16, f32 = jnp.bfloat16, jnp.float32
    operands = (kv_tiles.T, queries, keys.reshape(-1, TILE, columns), values.reshape(-1, TILE, columns), out_weight)
    return pl.pallas_call(
        functools.partial(kernel, devices, groups, chunk, late),
        out_shape=jax.ShapeDtypeStruct((rows, width), bf16),
        in_specs=[pl.BlockSpec(memory_space=pltpu.HBM)] * len(operands),
        out_specs=pl.BlockSpec(memory_space=pltpu.VMEM),
        scratch_shapes=[
            pltpu.SMEM(kv_tiles.shape[::-1], jnp.int32),
            pltpu.VMEM((tokens, columns), bf16),
            pltpu.VMEM((tokens // TILE, TILE, columns), bf16),
            pltpu.VMEM((tokens // TILE, TILE, columns), bf16),
            pltpu.VMEM((columns, width), bf16),
            pltpu.VMEM((tokens // TILE, 1, tokens + KINDS * PAIR * TILE), f32),
            pltpu.VMEM((heads, KINDS, 2 * PAIR * TILE, HD), bf16),
            pltpu.VMEM((heads, KINDS, 2 * PAIR * TILE, HD), bf16),
            pltpu.VMEM((heads, 2 * PAIR * TILE, HD), bf16),
            pltpu.VMEM((tokens, columns), bf16),
            pltpu.VMEM((2 * rows, deep * HD), bf16),
            pltpu.VMEM((chunks, deep * HD, chunk), bf16),
            pltpu.VMEM((len(set(late)), pairs - 1, rows, HD), bf16),
            pltpu.VMEM((HD, width), bf16),
            pltpu.VMEM((pairs - 1, chunks, rows, chunk), f32),
            pltpu.VMEM((pairs - 1, chunks, rows, chunk), bf16),
            pltpu.VMEM((pairs - 1, chunks, rows, chunk), bf16),
            pltpu.VMEM((pairs - 1, chunks, rows, chunk), bf16),
            pltpu.VMEM((pairs - 1, chunks, rows, chunk), bf16),
            pltpu.VMEM((chunks, 2 * rows, chunk), f32),
            pltpu.VMEM((chunks, rows, chunk), bf16),
            pltpu.VMEM((chunks, rows, chunk), bf16),
            sems((5,)),
            sems((heads, KINDS)), sems((heads, KINDS)),
            sems((heads,)), sems((heads,)), sems((heads,)), sems((heads,)),
            sems((chunks,)), sems((chunks,)),
            sems((deep,)), sems((deep,)),
            sems((len(set(late)), pairs - 1)), sems((len(set(late)), pairs - 1)),
            sems((len(set(late)),)), sems((len(set(late)),)),
            sems((pairs - 1, chunks)), sems((pairs - 1, chunks)),
            sems((pairs - 1, chunks)), sems((pairs - 1, chunks)),
            sems((chunks,)), sems((chunks,)),
        ],
        compiler_params=pltpu.CompilerParams(
            collective_id=0, has_side_effects=True, vmem_limit_bytes=40 * 2 ** 20),
    )(*[pltpu.with_memory_space_constraint(operand, pltpu.HBM) for operand in operands])


def solution(mesh):
    return jax.shard_map(
        body,
        mesh=mesh,
        in_specs=(P("ctx", "head"), P("ctx", "head"), P("ctx", "head"), P(), P("head", None)),
        out_specs=P(("ctx", "head"), None),
        check_vma=False,
    )
```
